256 devices in a mesh: gx: 64 (over z, x, core), gy: 4 (over y).
Axes of the slice: x: 4, y: 4, z: 8, core: 2. Of those that a mesh axis runs over, the one named last changes fastest.
Arguments:
- adjoint_block: float32 [4, 3, 64, 256, 512], P(None, None, None, 'gx', 'gy'), may hold values from -18 to 18
- base_flow: float32 [2, 3, 64, 256, 512], P(None, None, None, 'gx', 'gy'), may hold values from -4 to 4
- direct_modes: float32 [8, 3, 64, 256, 512], P(None, None, None, 'gx', 'gy'), may hold values from -0.0012207031 to 0.0012207031
- dual_modes: float32 [8, 3, 64, 256, 512], P(None, None, None, 'gx', 'gy'), may hold values from -0.6 to 0.6
Outputs:
- next_block: float32 [4, 3, 64, 256, 512], P(None, None, None, 'gx', 'gy')
- growth: float32 [4, 4], replicated
The draws below stay inside these ranges and needn't reach their ends.
All inputs are finite; a program needn't handle non-finite values.
Results may differ from the reference program's by a relative error of at most 0.0001.
Values sent between devices are 32-bit elements; how exact they have to be, the bound alone decides.
A program may use at most 128 MiB of HBM per device.

```python
import math
import jax
import jax.numpy as jnp
from jax import lax

NZ = 64
VECS = 4
MODES = 8
NX = 256
NY = 512


def draw_adjoint_block(key, part):
    shape = (VECS, 3, NZ, NX, NY)
    ramp = 1.0 + 2.0 * jnp.arange(NX, dtype=jnp.float32) / max(NX - 1, 1)
    values = jax.random.truncated_normal(key, -6.0, 6.0, shape, jnp.float32)
    return values * ramp[:, None]


def block_levels(own_key, extent, cuts, least, high):
    level, own = 1.0, jax.random.fold_in(own_key, 6)
    for axis_at, shards_of in cuts:
        steps = jnp.exp(jax.random.uniform(jax.random.fold_in(own, axis_at), (shards_of,), jnp.float32, least / len(cuts), high / len(cuts)))
        level = level * jnp.repeat(steps, extent[axis_at] // shards_of).reshape([-1 if axis == axis_at else 1 for axis in range(len(extent))])
    return level


def bell_draw(rng, shape, width, most, shards=(), kind=jnp.bfloat16):
    factor_of = block_levels(rng, shape, shards, -0.22, 0.18) if shards else 1.0
    values = jax.random.normal(rng, shape, jnp.float32) * width * factor_of
    return jnp.minimum(jnp.maximum(values, -most), most).astype(kind)


def setup_inputs(seed: int = 0) -> dict:
    keys = jax.random.split(jax.random.key(seed), 5)
    return {
        "adjoint_block": draw_adjoint_block(jax.random.fold_in(keys[4], 71), 0),
        "base_flow": bell_draw(keys[1], (2, 3, NZ, NX, NY), 1.0, 4.0, ((3, 64), (4, 4)), jnp.float32),
        "direct_modes": bell_draw(keys[2], (MODES, 3, NZ, NX, NY), (3 * NZ * NX * NY) ** -0.5, 0.0012207031, ((3, 64), (4, 4)), jnp.float32),
        "dual_modes": bell_draw(keys[3], (MODES, 3, NZ, NX, NY), 0.1, 0.6, ((3, 64), (4, 4)), jnp.float32),
    }


step_size = 0.1
viscosity = 0.2

def central_x(padded):
    return 0.5 * (padded[..., 2:, 1:-1] - padded[..., :-2, 1:-1])

def central_y(padded):
    return 0.5 * (padded[..., 1:-1, 2:] - padded[..., 1:-1, :-2])

def central_z(interior):
    return 0.5 * (jnp.roll(interior, -1, axis=-3) - jnp.roll(interior, 1, axis=-3))

def laplace(padded):
    interior = padded[..., 1:-1, 1:-1]
    beside_all = padded[..., 2:, 1:-1] + padded[..., :-2, 1:-1] + padded[..., 1:-1, 2:] + padded[..., 1:-1, :-2]
    beside_all = beside_all + jnp.roll(interior, -1, axis=-3) + jnp.roll(interior, 1, axis=-3)
    return beside_all - 6.0 * interior

def base_terms(padded_base):
    centre = padded_base[..., 1:-1, 1:-1]
    gradients = jnp.stack([central_x(padded_base), central_y(padded_base), central_z(centre)])
    return (centre, gradients)

def adjoint_step(padded, centre, gradients):
    interior = padded[..., 1:-1, 1:-1]
    advect = centre[0] * central_x(padded) + centre[1] * central_y(padded) + centre[2] * central_z(interior)
    produce = lax.optimization_barrier(jnp.sum(interior[:, None] * gradients[None], axis=2))
    return interior + step_size * (advect - produce + viscosity * laplace(padded))

def project(left, right):
    return lax.dot_general(left.astype(jnp.float32), right.astype(jnp.float32), (((1,), (1,)), ((), ())), precision=lax.Precision.HIGHEST, preferred_element_type=jnp.float32)

def combine_modes(coefficients, modes):
    return jnp.dot(coefficients.T.astype(jnp.float32), modes.astype(jnp.float32), precision=lax.Precision.HIGHEST, preferred_element_type=jnp.float32)

def pad_plane(field):
    return jnp.pad(field, [(0, 0)] * (field.ndim - 2) + [(1, 1), (1, 1)])

def reference(adjoint_block, base_flow, direct_modes, dual_modes):
    row_count = 3 * NZ * NX * NY
    direct_flat = direct_modes.reshape(MODES, row_count)
    dual_flat = dual_modes.reshape(MODES, row_count)
    current = adjoint_block
    for substep in range(2):
        centre, gradients = base_terms(pad_plane(base_flow[substep]))
        advanced = adjoint_step(pad_plane(current), centre, gradients)
        flattened = advanced.reshape(VECS, row_count)
        coefficients = project(direct_flat, flattened)
        flattened = flattened - combine_modes(coefficients, dual_flat)
        current = flattened.reshape(advanced.shape)
    gram_matrix = project(flattened, flattened)
    cholesky_factor = jnp.linalg.cholesky(gram_matrix)
    solved = jax.scipy.linalg.solve_triangular(cholesky_factor, flattened, lower=True)
    next_block = (math.sqrt(row_count) * solved).reshape(adjoint_block.shape)
    return (next_block, cholesky_factor)
```

```python
import functools
import math

import jax
import jax.numpy as jnp
from jax import lax
from jax.experimental import pallas as pl
from jax.experimental.pallas import tpu as pltpu
from jax.sharding import PartitionSpec as P

MESH = pl.DeviceIdType.MESH
F32 = jnp.float32
STEP = 0.1
VISC = 0.2
V, C, M = 4, 3, 8
XL, LN = 4, 128
CHIPS_X = 4
PAIRS_C = 32
PAIRS_FF = 32
PAIRS_UF = 42
PAIRS_UU = 74
PAIRS = 110


def kernel(
    n_gx, n_gy, nz, cells,
    q_hbm, b_hbm, d_hbm, u_hbm, out_hbm, growth_ref,
    q, b, d, u, a1, q1, f, out,
    xs, xr, bxs, bxr, ys, yr, bys, byr, w, wb,
    acc, ca, cb, coef, g1a, g1b, g2a, g2b,
    in_sem, out_sem, sx_sem, rx_sem, sy_sem, ry_sem, sg_sem, rg_sem,
):
    rows = nz * XL
    blocks = nz // 8
    nf = V * C
    gx, gy = lax.axis_index("gx"), lax.axis_index("gy")
    core = lax.rem(gx, 2)
    cx = lax.rem(lax.div(gx, 2), CHIPS_X)
    cz = lax.div(gx, 2 * CHIPS_X)
    n_z = n_gx // (2 * CHIPS_X)
    size_a, size_b = 2 * n_z, CHIPS_X * n_gy
    me_a, me_b = cz * 2 + core, cx * n_gy + gy

    def member_a(i):
        return ((lax.div(i, 2) * CHIPS_X + cx) * 2 + lax.rem(i, 2), gy)

    def member_b(i):
        return ((cz * CHIPS_X + lax.div(i, n_gy)) * 2 + core, lax.rem(i, n_gy))

    left, right = (lax.rem(gx + n_gx - 1, n_gx), gy), (lax.rem(gx + 1, n_gx), gy)
    below, above = (gx, lax.rem(gy + n_gy - 1, n_gy)), (gx, lax.rem(gy + 1, n_gy))
    has_l, has_r = gx > 0, gx < n_gx - 1
    has_b, has_a = gy > 0, gy < n_gy - 1

    q_main = pltpu.make_async_copy(q_hbm, q.at[:, pl.ds(8, rows), :], in_sem.at[0])
    q_low = pltpu.make_async_copy(q_hbm.at[:, pl.ds(rows - 8, 8), :], q.at[:, pl.ds(0, 8), :], in_sem.at[1])
    q_high = pltpu.make_async_copy(q_hbm.at[:, pl.ds(0, 8), :], q.at[:, pl.ds(rows + 8, 8), :], in_sem.at[2])
    b_main = pltpu.make_async_copy(b_hbm, b.at[:, pl.ds(8, rows), :], in_sem.at[3])
    b_low = pltpu.make_async_copy(b_hbm.at[:, pl.ds(rows - 8, 8), :], b.at[:, pl.ds(0, 8), :], in_sem.at[4])
    b_high = pltpu.make_async_copy(b_hbm.at[:, pl.ds(0, 8), :], b.at[:, pl.ds(rows + 8, 8), :], in_sem.at[5])
    u_main = pltpu.make_async_copy(u_hbm, u, in_sem.at[6])
    d_main = pltpu.make_async_copy(d_hbm, d, in_sem.at[7])
    q_main.start()
    b_main.start()
    for copy in (q_low, q_high, b_low, b_high, u_main, d_main):
        copy.start()

    barrier = pltpu.get_barrier_semaphore()
    for peer in (left, right, below, above):
        pl.semaphore_signal(barrier, inc=1, device_id=peer, device_id_type=MESH)

    @pl.loop(1, size_a)
    def _(step):
        pl.semaphore_signal(
            barrier, inc=1, device_id=member_a(lax.rem(me_a + step, size_a)), device_id_type=MESH
        )

    @pl.loop(1, size_b)
    def _(step):
        pl.semaphore_signal(
            barrier, inc=1, device_id=member_b(lax.rem(me_b + step, size_b)), device_id_type=MESH
        )

    lane = lax.broadcasted_iota(jnp.int32, (8, LN), 1)
    half = lax.shift_right_logical(lane, 1)
    first, final, odd = lane == 0, lane == LN - 1, lax.rem(lane, 2) == 1

    def plane(ref, field, k, x, dz=0, pad=8):
        return ref[field, pl.ds(pad + 8 * XL * k + x + XL * dz, 8, stride=XL), :]

    def zero(ref, count):
        @pl.loop(0, count)
        def _(i):
            ref[i] = jnp.zeros((nz, LN), F32)

    def x_copy(send, recv, side, sem):
        peer = left if side == 0 else right
        return pltpu.make_async_remote_copy(
            src_ref=send.at[side], dst_ref=recv.at[1 - side],
            send_sem=sx_sem.at[sem + side], recv_sem=rx_sem.at[sem + 1 - side],
            device_id=peer, device_id_type=MESH,
        )

    def x_start(send, recv, sem):
        for side, there in ((0, has_l), (1, has_r)):
            @pl.when(there)
            def _():
                x_copy(send, recv, side, sem).start()

    def x_wait(send, recv, sem, count):
        for side, there in ((0, has_l), (1, has_r)):
            @pl.when(there)
            def _():
                x_copy(send, recv, 1 - side, sem).wait_recv()

    def x_sent(send, recv, sem):
        for side, there in ((0, has_l), (1, has_r)):
            @pl.when(there)
            def _():
                x_copy(send, recv, side, sem).wait_send()

    def x_zero(recv, count):
        for side, there in ((0, has_l), (1, has_r)):
            @pl.when(jnp.logical_not(there))
            def _():
                zero(recv.at[side], count)

    def y_copy(send, recv, side, sem):
        peer = below if side == 0 else above
        return pltpu.make_async_remote_copy(
            src_ref=send, dst_ref=recv.at[1 - side],
            send_sem=sy_sem.at[sem + side], recv_sem=ry_sem.at[sem + 1 - side],
            device_id=peer, device_id_type=MESH,
        )

    def y_start(send, recv, sem):
        for side, there in ((0, has_b), (1, has_a)):
            @pl.when(there)
            def _():
                y_copy(send, recv, side, sem).start()

    def y_wait(send, recv, sem):
        for side, there in ((0, has_b), (1, has_a)):
            @pl.when(there)
            def _():
                y_copy(send, recv, 1 - side, sem).wait_recv()

    def y_sent(send, recv, sem):
        for side, there in ((0, has_b), (1, has_a)):
            @pl.when(there)
            def _():
                y_copy(send, recv, side, sem).wait_send()

    def y_zero(recv):
        for side, there in ((0, has_b), (1, has_a)):
            @pl.when(jnp.logical_not(there))
            def _():
                recv[side] = jnp.zeros((nz, LN), F32)

    def x_pack(ref, send, count):
        @pl.loop(0, count)
        def _(i):
            for k in range(blocks):
                at = pl.ds(8 * k, 8)
                send[0, i, at, :] = plane(ref, i, k, 0)
                send[1, i, at, :] = plane(ref, i, k, XL - 1)

    def y_pack(ref, send, count):
        @pl.loop(0, blocks)
        def _(k):
            total = jnp.zeros((8, LN), F32)
            for x in range(XL):
                for i in range(count):
                    at = 16 * x + i
                    total = jnp.where(half == at, pltpu.roll(plane(ref, i, k, x), 2 * at + 1, 1), total)
            send[pl.ds(pl.multiple_of(8 * k, 8), 8), :] = total

    def y_merge(recv, merged):
        for k in range(blocks):
            at = pl.ds(8 * k, 8)
            merged[at, :] = jnp.where(
                odd, pltpu.roll(recv[0, at, :], 1, 1), pltpu.roll(recv[1, at, :], LN - 1, 1)
            )

    def beside_y(value, edges, x, field):
        fix = pltpu.roll(edges, LN - (32 * x + 2 * field + 1), 1)
        return (
            jnp.where(first, fix, pltpu.roll(value, 1, 1)),
            jnp.where(final, fix, pltpu.roll(value, LN - 1, 1)),
        )

    def beside_x(ref, recv, field, k, x):
        at = pl.ds(pl.multiple_of(8 * k, 8), 8)
        low = recv[0, field, at, :] if x == 0 else plane(ref, field, k, x - 1)
        high = recv[1, field, at, :] if x == XL - 1 else plane(ref, field, k, x + 1)
        return low, high

    def stencil(src, src_x, edges, s, dst, planes):
        @pl.loop(0, blocks)
        def _(k):
            at = pl.ds(pl.multiple_of(8 * k, 8), 8)
            wk, wbk = edges[at, :], wb[at, :]
            for x in planes:
                base = [plane(b, 3 * s + j, k, x) for j in range(C)]
                low = [VISC * STEP - 0.5 * STEP * t for t in base]
                high = [VISC * STEP + 0.5 * STEP * t for t in base]
                mix = [[None] * C for _ in range(C)]
                for j in range(C):
                    field = 3 * s + j
                    xm, xp = beside_x(b, bxr, field, k, x)
                    ym, yp = beside_y(base[j], wbk, x, field)
                    zm, zp = plane(b, field, k, x, -1), plane(b, field, k, x, 1)
                    for c, (m_, p_) in enumerate(((xm, xp), (ym, yp), (zm, zp))):
                        mix[c][j] = 0.5 * STEP * (m_ - p_)
                for c in range(C):
                    mix[c][c] = mix[c][c] + (1.0 - 6.0 * VISC * STEP)
                for v in range(V):
                    mid = [plane(src, C * v + c, k, x) for c in range(C)]
                    for c in range(C):
                        field = C * v + c
                        xm, xp = beside_x(src, src_x, field, k, x)
                        ym, yp = beside_y(mid[c], wk, x, field)
                        zm, zp = plane(src, field, k, x, -1), plane(src, field, k, x, 1)
                        total = mix[c][0] * mid[0] + mix[c][1] * mid[1] + mix[c][2] * mid[2]
                        total = total + (low[0] * xm + high[0] * xp)
                        total = total + (low[1] * ym + high[1] * yp)
                        total = total + (low[2] * zm + high[2] * zp)
                        dst[field, pl.ds(8 * XL * k + x, 8, stride=XL), :] = total

    def pair_sums(start, pairs, loader):
        zeros = tuple(jnp.zeros((8, LN), F32) for _ in pairs)

        def body(t, sums):
            sums = list(sums)
            at = pl.ds(pl.multiple_of(8 * t, 8), 8)
            for c in range(C):
                left_, right_ = loader(c, at)
                for n, (i, j) in enumerate(pairs):
                    sums[n] = sums[n] + left_[i] * right_[j]
            return tuple(sums)

        sums = lax.fori_loop(0, rows // 8, body, zeros)
        for n, value in enumerate(sums):
            acc[pl.ds(start + n, 1), :] = jnp.sum(value, axis=0, keepdims=True)

    ones = jnp.ones((8, LN), F32)

    def all_reduce(part_a, part_b, row, which):
        def stage(buf, size, me, member, sem):
            def copy(i, peer):
                return pltpu.make_async_remote_copy(
                    src_ref=buf.at[i], dst_ref=buf.at[i],
                    send_sem=sg_sem.at[sem], recv_sem=rg_sem.at[sem],
                    device_id=peer, device_id_type=MESH,
                )

            @pl.loop(1, size)
            def _(step):
                copy(me, member(lax.rem(me + step, size))).start()

            everything = pltpu.make_async_remote_copy(
                src_ref=buf.at[pl.ds(0, size - 1)], dst_ref=buf.at[pl.ds(0, size - 1)],
                send_sem=sg_sem.at[sem], recv_sem=rg_sem.at[sem],
                device_id=member(lax.rem(me + 1, size)), device_id_type=MESH,
            )
            everything.wait_recv()
            everything.wait_send()
            total = buf[0]
            for i in range(1, size):
                total = total + buf[i]
            return total

        part_a[me_a] = row
        part_b[me_b] = stage(part_a, size_a, me_a, member_a, 2 * which)
        return stage(part_b, size_b, me_b, member_b, 2 * which + 1)

    def lane_sums():
        return lax.dot_general(
            ones, acc[...], (((1,), (1,)), ((), ())),
            precision=lax.Precision.HIGHEST, preferred_element_type=F32,
        )[0:1, :]

    def spread(row, count, dst):
        r = lax.broadcasted_iota(jnp.int32, (count, LN), 0)
        l = lax.broadcasted_iota(jnp.int32, (count, LN), 1)
        chosen = jnp.where(r == l, jnp.broadcast_to(row, (count, LN)), 0.0)
        dst[pl.ds(0, count), :] = lax.dot_general(
            chosen, jnp.ones((LN, LN), F32), (((1,), (0,)), ((), ())),
            precision=lax.Precision.HIGHEST, preferred_element_type=F32,
        )

    q_main.wait()
    x_pack(q, xs.at[0], nf)
    b_main.wait()
    x_pack(b, bxs, 2 * C)
    pl.semaphore_wait(barrier, 4 + (size_a - 1) + (size_b - 1))
    x_start(xs.at[0], xr.at[0], 0)
    y_pack(q, ys.at[0], nf)
    y_start(ys.at[0], yr.at[0], 0)
    x_start(bxs, bxr, 2)
    y_pack(b, bys, 2 * C)
    y_start(bys, byr, 2)
    x_zero(xr.at[0], nf)
    x_zero(xr.at[1], nf)
    x_zero(bxr, 2 * C)
    y_zero(yr.at[0])
    y_zero(yr.at[1])
    y_zero(byr)
    for copy in (q_low, q_high, b_low, b_high, u_main):
        copy.wait()

    acc[...] = jnp.zeros((LN, LN), F32)
    uu = [(i, j) for i in range(M) for j in range(i, M)]

    def load_uu(c, at):
        rows_ = [u[C * i + c, at, :] for i in range(M)]
        return rows_, rows_

    pair_sums(PAIRS_UU, uu, load_uu)

    y_wait(ys.at[0], yr.at[0], 0)
    y_wait(bys, byr, 2)
    y_merge(yr.at[0], w)
    y_merge(byr, wb)
    stencil(q, xr.at[0], w, 0, a1, (1, 2))
    x_wait(xs.at[0], xr.at[0], 0, nf)
    x_wait(bxs, bxr, 2, 2 * C)
    stencil(q, xr.at[0], w, 0, a1, (0, 3))
    d_main.wait()

    modes_by_vectors = [(m, i) for m in range(M) for i in range(V)]

    def load_da(field):
        def loader(c, at):
            return [d[C * m + c, at, :] for m in range(M)], [field[C * i + c, at, :] for i in range(V)]
        return loader

    pair_sums(0, modes_by_vectors, load_da(a1))
    row1 = all_reduce(g1a, g1b, lane_sums(), 0)
    spread(row1, PAIRS_C, ca)

    def deflate(planes, send):
        @pl.loop(0, blocks)
        def _(k):
            at = pl.ds(pl.multiple_of(8 * k, 8), 8)
            for c in range(C):
                for x in planes:
                    dual = [plane(u, C * m + c, k, x, 0, 0) for m in range(M)]
                    for i in range(V):
                        field = C * i + c
                        total = plane(a1, field, k, x, 0, 0)
                        for m in range(M):
                            total = total - ca[pl.ds(V * m + i, 1), :] * dual[m]
                        q1[field, pl.ds(8 + 8 * XL * k + x, 8, stride=XL), :] = total
                        if send:
                            xs[1, 0 if x == 0 else 1, field, at, :] = total

    deflate((0, 3), True)
    x_start(xs.at[1], xr.at[1], 4)
    deflate((1, 2), False)
    y_pack(q1, ys.at[1], nf)
    y_start(ys.at[1], yr.at[1], 4)
    for field in range(nf):
        q1[field, pl.ds(0, 8), :] = q1[field, pl.ds(rows, 8), :]
        q1[field, pl.ds(rows + 8, 8), :] = q1[field, pl.ds(8, 8), :]
    y_wait(ys.at[1], yr.at[1], 4)
    y_merge(yr.at[1], w)
    stencil(q1, xr.at[1], w, 1, f, (1, 2))
    x_wait(xs.at[1], xr.at[1], 4, nf)
    stencil(q1, xr.at[1], w, 1, f, (0, 3))

    pair_sums(0, modes_by_vectors, load_da(f))
    tri = [(i, j) for i in range(V) for j in range(i, V)]

    def load_f(c, at):
        both = [f[C * i + c, at, :] for i in range(V)]
        both = both + [u[C * m + c, at, :] for m in range(M)]
        return both, both

    pair_sums(PAIRS_FF, tri + [(V + m, i) for m in range(M) for i in range(V)], load_f)
    row2 = all_reduce(g2a, g2b, lane_sums(), 1)
    spread(row2, 112, cb)

    def val(n):
        return cb[pl.ds(n, 1), :]

    c2 = [[val(V * m + i) for i in range(V)] for m in range(M)]
    ff, uf, dd = {}, {}, {}
    for n, (i, j) in enumerate(tri):
        ff[i, j] = val(PAIRS_FF + n)
    for m in range(M):
        for i in range(V):
            uf[m, i] = val(PAIRS_UF + V * m + i)
    for n, (i, j) in enumerate(uu):
        dd[i, j] = dd[j, i] = val(PAIRS_UU + n)

    def total_of(terms):
        terms = list(terms)
        while len(terms) > 1:
            terms = [
                terms[i] + terms[i + 1] if i + 1 < len(terms) else terms[i] for i in range(0, len(terms), 2)
            ]
        return terms[0]

    gram = {}
    for j in range(V):
        h = [total_of(dd[m, n] * c2[n][j] for n in range(M)) - uf[m, j] for m in range(M)]
        for i in range(j, V):
            gram[i, j] = ff[j, i] + total_of(c2[m][i] * h[m] - c2[m][j] * uf[m, i] for m in range(M))
    low = {}
    inv = {}
    for j in range(V):
        pivot = gram[j, j]
        for k in range(j):
            pivot = pivot - low[j, k] * low[j, k]
        low[j, j] = jnp.sqrt(pivot)
        inv[j, j] = 1.0 / low[j, j]
        for i in range(j + 1, V):
            total = gram[i, j]
            for k in range(j):
                total = total - low[i, k] * low[j, k]
            low[i, j] = total * inv[j, j]
    for i in range(V):
        for j in range(i):
            total = low[i, j] * inv[j, j]
            for k in range(j + 1, i):
                total = total + low[i, k] * inv[k, j]
            inv[i, j] = -total * inv[i, i]
    lane1 = lax.broadcasted_iota(jnp.int32, (1, LN), 1)
    for i in range(V):
        row = jnp.zeros((1, LN), F32)
        for j in range(i + 1):
            row = jnp.where(lane1 == j, low[i, j], row)
        growth_ref[pl.ds(i, 1), :] = row[:, 0:V]
    scale = math.sqrt(cells)
    slot = {}
    n = 0
    for i in range(V):
        for j in range(i + 1):
            coef[pl.ds(n, 1), :] = scale * inv[i, j]
            slot["f", i, j] = n
            n += 1
    for i in range(V):
        for m in range(M):
            coef[pl.ds(n, 1), :] = -scale * total_of(inv[i, j] * c2[m][j] for j in range(i + 1))
            slot["u", i, m] = n
            n += 1

    for c in range(C):
        @pl.loop(0, rows // 8)
        def _(t):
            at = pl.ds(pl.multiple_of(8 * t, 8), 8)
            fs = [f[C * i + c, at, :] for i in range(V)]
            us = [u[C * m + c, at, :] for m in range(M)]
            for i in range(V):
                terms = [coef[pl.ds(slot["f", i, j], 1), :] * fs[j] for j in range(i + 1)]
                terms += [coef[pl.ds(slot["u", i, m], 1), :] * us[m] for m in range(M)]
                out[C * i + c, at, :] = total_of(terms)

        for i in range(V):
            pltpu.make_async_copy(out.at[C * i + c], out_hbm.at[C * i + c], out_sem.at[C * i + c]).start()
    for n in range(nf):
        pltpu.make_async_copy(out.at[n], out_hbm.at[n], out_sem.at[n]).wait()
    x_sent(xs.at[0], xr.at[0], 0)
    x_sent(bxs, bxr, 2)
    x_sent(xs.at[1], xr.at[1], 4)
    y_sent(ys.at[0], yr.at[0], 0)
    y_sent(bys, byr, 2)
    y_sent(ys.at[1], yr.at[1], 4)


def body(n_gx, n_gy, adjoint_block, base_flow, direct_modes, dual_modes):
    nz = adjoint_block.shape[2]
    rows = nz * XL
    cells = float(C * nz * XL * n_gx * LN * n_gy)
    nf = V * C
    size_a, size_b = 2 * (n_gx // (2 * CHIPS_X)), CHIPS_X * n_gy
    vm = lambda *shape: pltpu.VMEM(shape, F32)
    anyspace = pl.BlockSpec(memory_space=pltpu.HBM)
    out, growth = pl.pallas_call(
        functools.partial(kernel, n_gx, n_gy, nz, cells),
        name="adjoint_step",
        out_shape=(
            jax.ShapeDtypeStruct((nf, rows, LN), F32),
            jax.ShapeDtypeStruct((V, V), F32),
        ),
        in_specs=[anyspace] * 4,
        out_specs=(anyspace, pl.BlockSpec(memory_space=pltpu.VMEM)),
        scratch_shapes=[
            vm(nf, rows + 16, LN), vm(2 * C, rows + 16, LN), vm(M * C, rows, LN), vm(M * C, rows, LN),
            vm(nf, rows, LN), vm(nf, rows + 16, LN), vm(nf, rows, LN), vm(nf, rows, LN),
            vm(2, 2, nf, nz, LN), vm(2, 2, nf, nz, LN), vm(2, 2 * C, nz, LN), vm(2, 2 * C, nz, LN),
            vm(2, nz, LN), vm(2, 2, nz, LN), vm(nz, LN), vm(2, nz, LN), vm(nz, LN), vm(nz, LN),
            vm(LN, LN), vm(PAIRS_C, LN), vm(112, LN), vm(48, LN),
            vm(size_a, 1, LN), vm(size_b, 1, LN), vm(size_a, 1, LN), vm(size_b, 1, LN),
            pltpu.SemaphoreType.DMA((8,)), pltpu.SemaphoreType.DMA((nf,)),
            pltpu.SemaphoreType.DMA((6,)), pltpu.SemaphoreType.DMA((6,)),
            pltpu.SemaphoreType.DMA((6,)), pltpu.SemaphoreType.DMA((6,)),
            pltpu.SemaphoreType.DMA((4,)), pltpu.SemaphoreType.DMA((4,)),
        ],
        compiler_params=pltpu.CompilerParams(
            collective_id=0, has_side_effects=True, vmem_limit_bytes=48 * 1024 * 1024
        ),
    )(
        adjoint_block.reshape(nf, rows, LN),
        base_flow.reshape(2 * C, rows, LN),
        direct_modes.reshape(M * C, rows, LN),
        dual_modes.reshape(M * C, rows, LN),
    )
    return out.reshape(adjoint_block.shape), growth


def solution(mesh):
    spec = P(None, None, None, "gx", "gy")
    return jax.shard_map(
        functools.partial(body, mesh.shape["gx"], mesh.shape["gy"]),
        mesh=mesh,
        in_specs=(spec,) * 4,
        out_specs=(spec, P()),
        check_vma=False,
    )
```

```python
import functools
import math

import jax
import jax.numpy as jnp
from jax import lax
from jax.experimental import pallas as pl
from jax.experimental.pallas import tpu as pltpu
from jax.sharding import PartitionSpec as P

MESH = pl.DeviceIdType.MESH
F32 = jnp.float32
STEP = 0.1
VISC = 0.2
V, C, M = 4, 3, 8
XL, LN = 4, 128
CHIPS_X = 4
PAIRS_C = 32
PAIRS_FF = 32
PAIRS_UF = 42
PAIRS_UU = 74
PAIRS = 110


def kernel(
    n_gx, n_gy, nz, cells,
    q_hbm, b_hbm, d_hbm, u_hbm, out, growth_ref,
    q, b, d, u, a1, q1, f, terms, part,
    xs, xr, bxs, bxr, ys, yr, bys, byr, w, wb,
    acc, ca, cb, coef, g1, g2,
    in_sem, sx_sem, rx_sem, sy_sem, ry_sem, sg_sem, rg_sem, known,
):
    rows = nz * XL
    blocks = nz // 8
    nf = V * C
    gx, gy = lax.axis_index("gx"), lax.axis_index("gy")
    core = lax.rem(gx, 2)
    cx = lax.rem(lax.div(gx, 2), CHIPS_X)
    cz = lax.div(gx, 2 * CHIPS_X)
    n_z = n_gx // (2 * CHIPS_X)
    size_a, size_b = 2 * n_z, CHIPS_X * n_gy
    me_a, me_b = cz * 2 + core, cx * n_gy + gy

    def ring(size):
        return sorted(range(1, size), key=lambda s: -min(s, size - s)) + [0]

    zs = [lax.rem(cz + s, n_z) if s else cz for s in ring(n_z)]
    peers_a = [
        ((z * CHIPS_X + cx) * 2 + c, gy) for z in zs for c in (1 - core, core)
    ][: size_a - 1]
    xs_, ys_ = (
        [lax.rem(cx + s, CHIPS_X) if s else cx for s in ring(CHIPS_X)],
        [lax.rem(gy + s, n_gy) if s else gy for s in ring(n_gy)],
    )
    peers_b = [((cz * CHIPS_X + x) * 2 + core, y) for x in xs_ for y in ys_][: size_b - 1]

    def hops(size, n):
        s = (ring(size))[n]
        return min(s, size - s)

    order = sorted(
        (
            (i, j, k, n)
            for i in range(n_z) for j in range(CHIPS_X) for k in range(n_gy) for n in range(2)
        ),
        key=lambda t: -(4 * (hops(n_z, t[0]) + hops(CHIPS_X, t[1]) + hops(n_gy, t[2])) + (t[3] == 0)),
    )[:-1]
    peers_all = [
        ((zs[i] * CHIPS_X + xs_[j]) * 2 + (1 - core if n == 0 else core), ys_[k]) for i, j, k, n in order
    ]

    left, right = (lax.rem(gx + n_gx - 1, n_gx), gy), (lax.rem(gx + 1, n_gx), gy)
    below, above = (gx, lax.rem(gy + n_gy - 1, n_gy)), (gx, lax.rem(gy + 1, n_gy))
    has_l, has_r = gx > 0, gx < n_gx - 1
    has_b, has_a = gy > 0, gy < n_gy - 1

    def total_of(terms):
        terms = list(terms)
        while len(terms) > 1:
            terms = [
                terms[i] + terms[i + 1] if i + 1 < len(terms) else terms[i] for i in range(0, len(terms), 2)
            ]
        return terms[0]

    q_main = pltpu.make_async_copy(q_hbm, q.at[:, pl.ds(8, rows), :], in_sem.at[0])
    q_low = pltpu.make_async_copy(q_hbm.at[:, pl.ds(rows - 8, 8), :], q.at[:, pl.ds(0, 8), :], in_sem.at[1])
    q_high = pltpu.make_async_copy(q_hbm.at[:, pl.ds(0, 8), :], q.at[:, pl.ds(rows + 8, 8), :], in_sem.at[2])
    b_main = pltpu.make_async_copy(b_hbm, b.at[:, pl.ds(8, rows), :], in_sem.at[3])
    b_low = pltpu.make_async_copy(b_hbm.at[:, pl.ds(rows - 8, 8), :], b.at[:, pl.ds(0, 8), :], in_sem.at[4])
    b_high = pltpu.make_async_copy(b_hbm.at[:, pl.ds(0, 8), :], b.at[:, pl.ds(rows + 8, 8), :], in_sem.at[5])
    u_main = pltpu.make_async_copy(u_hbm, u, in_sem.at[6])
    d_main = pltpu.make_async_copy(d_hbm, d, in_sem.at[7])
    q_main.start()
    b_main.start()
    for copy in (q_low, q_high, b_low, b_high, u_main, d_main):
        copy.start()

    barrier = pltpu.get_barrier_semaphore()
    for peer in (left, right, below, above):
        pl.semaphore_signal(barrier, inc=1, device_id=peer, device_id_type=MESH)

    for peer in peers_a + peers_b:
        pl.semaphore_signal(barrier, inc=1, device_id=peer, device_id_type=MESH)

    lane = lax.broadcasted_iota(jnp.int32, (8, LN), 1)
    half = lax.shift_right_logical(lane, 1)
    first, final, odd = lane == 0, lane == LN - 1, lax.rem(lane, 2) == 1

    def plane(ref, field, k, x, dz=0, pad=8):
        return ref[field, pl.ds(pad + 8 * XL * k + x + XL * dz, 8, stride=XL), :]

    def zero(ref, count):
        @pl.loop(0, count)
        def _(i):
            ref[i] = jnp.zeros((nz, LN), F32)

    def x_copy(send, recv, fields, side, sem):
        peer = left if side == 0 else right
        return pltpu.make_async_remote_copy(
            src_ref=send.at[side, fields], dst_ref=recv.at[1 - side, fields],
            send_sem=sx_sem.at[sem + side], recv_sem=rx_sem.at[sem + 1 - side],
            device_id=peer, device_id_type=MESH,
        )

    def x_each(act):
        for side, there in ((0, has_l), (1, has_r)):
            @pl.when(there)
            def _():
                act(side)

    def x_start(send, recv, fields, sem):
        x_each(lambda side: x_copy(send, recv, fields, side, sem).start())

    def x_wait(send, recv, fields, sem):
        x_each(lambda side: x_copy(send, recv, fields, 1 - side, sem).wait_recv())

    def x_sent(send, recv, fields, sem):
        x_each(lambda side: x_copy(send, recv, fields, side, sem).wait_send())

    def x_zero(recv, count):
        for side, there in ((0, has_l), (1, has_r)):
            @pl.when(jnp.logical_not(there))
            def _():
                zero(recv.at[side], count)

    def y_copy(send, recv, side, sem):
        peer = below if side == 0 else above
        return pltpu.make_async_remote_copy(
            src_ref=send, dst_ref=recv.at[1 - side],
            send_sem=sy_sem.at[sem + side], recv_sem=ry_sem.at[sem + 1 - side],
            device_id=peer, device_id_type=MESH,
        )

    def y_start(send, recv, sem):
        for side, there in ((0, has_b), (1, has_a)):
            @pl.when(there)
            def _():
                y_copy(send, recv, side, sem).start()

    def y_wait(send, recv, sem):
        for side, there in ((0, has_b), (1, has_a)):
            @pl.when(there)
            def _():
                y_copy(send, recv, 1 - side, sem).wait_recv()

    def y_sent(send, recv, sem):
        for side, there in ((0, has_b), (1, has_a)):
            @pl.when(there)
            def _():
                y_copy(send, recv, side, sem).wait_send()

    def y_zero(recv):
        for side, there in ((0, has_b), (1, has_a)):
            @pl.when(jnp.logical_not(there))
            def _():
                recv[side] = jnp.zeros((nz, LN), F32)

    def x_pack(ref, send, count):
        @pl.loop(0, count)
        def _(i):
            for k in range(blocks):
                at = pl.ds(8 * k, 8)
                send[0, i, at, :] = plane(ref, i, k, 0)
                send[1, i, at, :] = plane(ref, i, k, XL - 1)

    def y_pack(ref, send, count):
        @pl.loop(0, blocks)
        def _(k):
            total = jnp.zeros((8, LN), F32)
            for x in range(XL):
                for i in range(count):
                    at = 16 * x + i
                    total = jnp.where(half == at, pltpu.roll(plane(ref, i, k, x), 2 * at + 1, 1), total)
            send[pl.ds(pl.multiple_of(8 * k, 8), 8), :] = total

    def y_merge(recv, merged):
        for k in range(blocks):
            at = pl.ds(8 * k, 8)
            merged[at, :] = jnp.where(
                odd, pltpu.roll(recv[0, at, :], 1, 1), pltpu.roll(recv[1, at, :], LN - 1, 1)
            )

    def beside_y(value, edges, x, field):
        fix = pltpu.roll(edges, LN - (32 * x + 2 * field + 1), 1)
        return (
            jnp.where(first, fix, pltpu.roll(value, 1, 1)),
            jnp.where(final, fix, pltpu.roll(value, LN - 1, 1)),
        )

    def beside_x(ref, recv, field, k, x):
        at = pl.ds(pl.multiple_of(8 * k, 8), 8)
        low = recv[0, field, at, :] if x == 0 else plane(ref, field, k, x - 1)
        high = recv[1, field, at, :] if x == XL - 1 else plane(ref, field, k, x + 1)
        return low, high

    def base_terms(s, planes):
        @pl.loop(0, blocks)
        def _(k):
            wbk = wb[pl.ds(pl.multiple_of(8 * k, 8), 8), :]
            for x in planes:
                at = pl.ds(pl.multiple_of(8 * k, 8) + nz * x, 8)
                mix = [[None] * C for _ in range(C)]
                for j in range(C):
                    field = 3 * s + j
                    mid = plane(b, field, k, x)
                    xm, xp = beside_x(b, bxr, field, k, x)
                    ym, yp = beside_y(mid, wbk, x, field)
                    zm, zp = plane(b, field, k, x, -1), plane(b, field, k, x, 1)
                    for c, (m_, p_) in enumerate(((xm, xp), (ym, yp), (zm, zp))):
                        mix[c][j] = 0.5 * STEP * (m_ - p_)
                    terms[s, 2 * j, at, :] = VISC * STEP - 0.5 * STEP * mid
                    terms[s, 2 * j + 1, at, :] = VISC * STEP + 0.5 * STEP * mid
                for c in range(C):
                    for j in range(C):
                        extra = 1.0 - 6.0 * VISC * STEP if c == j else 0.0
                        terms[s, 6 + C * c + j, at, :] = mix[c][j] + extra if extra else mix[c][j]

    def stencil(src, src_x, edges, s, dst, planes, vectors):
        @pl.loop(0, blocks)
        def _(k):
            wk = edges[pl.ds(pl.multiple_of(8 * k, 8), 8), :]
            for x in planes:
                at = pl.ds(pl.multiple_of(8 * k, 8) + nz * x, 8)
                side = [terms[s, n, at, :] for n in range(6)]
                mix = [[terms[s, 6 + C * c + j, at, :] for j in range(C)] for c in range(C)]
                for v in vectors:
                    mid = [plane(src, C * v + c, k, x) for c in range(C)]
                    for c in range(C):
                        field = C * v + c
                        xm, xp = beside_x(src, src_x, field, k, x)
                        ym, yp = beside_y(mid[c], wk, x, field)
                        zm, zp = plane(src, field, k, x, -1), plane(src, field, k, x, 1)
                        total = mix[c][0] * mid[0] + mix[c][1] * mid[1] + mix[c][2] * mid[2]
                        total = total + (side[0] * xm + side[1] * xp)
                        total = total + (side[2] * ym + side[3] * yp)
                        total = total + (side[4] * zm + side[5] * zp)
                        dst[field, pl.ds(8 * XL * k + x, 8, stride=XL), :] = total

    def pair_sums(pairs, loader, planes, fresh):
        def body(k, sums):
            sums = list(sums)
            for x in planes:
                at = pl.ds(8 * XL * k + x, 8, stride=XL)
                for c in range(C):
                    left_, right_ = loader(c, at)
                    for n, (_, i, j) in enumerate(pairs):
                        sums[n] = sums[n] + left_[i] * right_[j]
            return tuple(sums)

        begin = tuple(jnp.zeros((8, LN), F32) if fresh else part[n] for n, _, _ in pairs)
        for (n, _, _), value in zip(pairs, lax.fori_loop(0, blocks, body, begin)):
            part[n] = value

    def on_modes(vectors, field):
        pairs = [(V * m + i, m, n) for n, i in enumerate(vectors) for m in range(M)]

        def loader(c, at):
            return [d[C * m + c, at, :] for m in range(M)], [field[C * i + c, at, :] for i in vectors]

        return pairs, loader

    tri = [(i, j) for i in range(V) for j in range(i, V)]
    uu = [(i, j) for i in range(M) for j in range(i, M)]

    def on_duals(vectors, field):
        count = vectors[-1] + 1
        pairs = [(PAIRS_FF + n, M + i, j) for n, (i, j) in enumerate(tri) if j in vectors]
        pairs += [(PAIRS_UF + V * m + i, m, i) for m in range(M) for i in vectors]

        def loader(c, at):
            fs = [field[C * i + c, at, :] for i in range(count)]
            return [u[C * m + c, at, :] for m in range(M)] + fs, fs

        return pairs, loader

    def among_duals():
        def loader(c, at):
            both = [u[C * m + c, at, :] for m in range(M)]
            return both, both

        return [(PAIRS_UU + n, i, j) for n, (i, j) in enumerate(uu)], loader

    def fold(start, count):
        for n in range(start, start + count):
            acc[pl.ds(n, 1), :] = jnp.sum(part[n], axis=0, keepdims=True)

    ones = jnp.ones((8, LN), F32)

    def all_reduce(buf, row, sem, fill=None):
        me = gx * n_gy + gy
        size = n_gx * n_gy
        buf[me] = row

        def copy(rows_, peer):
            return pltpu.make_async_remote_copy(
                src_ref=buf.at[rows_], dst_ref=buf.at[rows_],
                send_sem=sg_sem.at[sem], recv_sem=rg_sem.at[sem],
                device_id=peer, device_id_type=MESH,
            )

        for peer in peers_all:
            copy(me, peer).start()
        if fill is not None:
            fill()
        copy(pl.ds(0, size - 1), peers_all[0]).wait_recv()
        sums = total_of([total_of(buf[i + k] for k in range(16)) for i in range(0, size, 16)])
        return sums, copy(pl.ds(0, size - 1), peers_all[0])

    def lane_sums():
        return lax.dot_general(
            ones, acc[...], (((1,), (1,)), ((), ())),
            precision=lax.Precision.HIGHEST, preferred_element_type=F32,
        )[0:1, :]

    def spread(row, count, dst):
        r = lax.broadcasted_iota(jnp.int32, (count, LN), 0)
        l = lax.broadcasted_iota(jnp.int32, (count, LN), 1)
        chosen = jnp.where(r == l, jnp.broadcast_to(row, (count, LN)), 0.0)
        dst[pl.ds(0, count), :] = lax.dot_general(
            chosen, jnp.ones((LN, LN), F32), (((1,), (0,)), ((), ())),
            precision=lax.Precision.HIGHEST, preferred_element_type=F32,
        )

    everything = (1, 2, 0, 3)
    inner, outer = (1, 2), (0, 3)
    chunks = ((0, 1), (2, 3))
    fields_of = [pl.ds(C * c[0], C * len(c)) for c in chunks]
    snapshot = [pl.ds(C * s, C) for s in range(2)]
    q_main.wait()
    x_pack(q, xs.at[0], nf)
    b_main.wait()
    x_pack(b, bxs, 2 * C)
    pl.semaphore_wait(barrier, 4 + len(peers_a) + len(peers_b))
    x_start(bxs, bxr, snapshot[0], 0)
    for n, fields in enumerate(fields_of):
        x_start(xs.at[0], xr.at[0], fields, 4 + 2 * n)
    x_start(bxs, bxr, snapshot[1], 2)
    for peer in peers_a:
        pl.semaphore_signal(known, inc=1, device_id=peer, device_id_type=MESH)
    y_pack(b, bys, 2 * C)
    y_start(bys, byr, 2)
    y_pack(q, ys.at[0], nf)
    y_start(ys.at[0], yr.at[0], 0)
    acc[...] = jnp.zeros((LN, LN), F32)
    x_zero(xr.at[0], nf)
    x_zero(xr.at[1], nf)
    x_zero(bxr, 2 * C)
    y_zero(yr.at[0])
    y_zero(yr.at[1])
    y_zero(byr)
    for copy in (q_low, q_high, b_low, b_high):
        copy.wait()
    y_wait(bys, byr, 2)
    y_merge(byr, wb)
    base_terms(0, inner)
    y_wait(ys.at[0], yr.at[0], 0)
    y_merge(yr.at[0], w)
    stencil(q, xr.at[0], w, 0, a1, inner, range(V))
    d_main.wait()

    pair_sums(*on_modes(tuple(range(V)), a1), inner, True)
    x_wait(bxs, bxr, snapshot[0], 0)
    base_terms(0, outer)
    for n, fields in enumerate(fields_of):
        x_wait(xs.at[0], xr.at[0], fields, 4 + 2 * n)
        stencil(q, xr.at[0], w, 0, a1, outer, chunks[n])
    pair_sums(*on_modes(tuple(range(V)), a1), outer, False)
    fold(0, PAIRS_C)

    def second_base():
        x_wait(bxs, bxr, snapshot[1], 2)
        base_terms(1, everything)

    def dual_products():
        u_main.wait()
        pair_sums(*among_duals(), everything, True)

    def shadow():
        second_base()
        dual_products()

    pl.semaphore_wait(known, len(peers_a))
    row1, sent1 = all_reduce(g1, lane_sums(), 0, shadow)
    fold(PAIRS_UU, len(uu))
    spread(row1, PAIRS_C, ca)

    def deflate(planes, vectors, send):
        weight = {
            (m, i): jnp.broadcast_to(ca[pl.ds(V * m + i, 1), :], (8, LN)) for m in range(M) for i in vectors
        }

        @pl.loop(0, blocks)
        def _(k):
            at = pl.ds(pl.multiple_of(8 * k, 8), 8)
            for c in range(C):
                for x in planes:
                    dual = [plane(u, C * m + c, k, x, 0, 0) for m in range(M)]
                    for i in vectors:
                        field = C * i + c
                        total = plane(a1, field, k, x, 0, 0) - total_of(weight[m, i] * dual[m] for m in range(M))
                        q1[field, pl.ds(8 + 8 * XL * k + x, 8, stride=XL), :] = total
                        if send:
                            xs[1, 0 if x == 0 else 1, field, at, :] = total

    for n, fields in enumerate(fields_of):
        deflate(outer, chunks[n], True)
        x_start(xs.at[1], xr.at[1], fields, 12 + 2 * n)
    deflate(inner, range(V), False)
    y_pack(q1, ys.at[1], nf)
    y_start(ys.at[1], yr.at[1], 4)
    for field in range(nf):
        q1[field, pl.ds(0, 8), :] = q1[field, pl.ds(rows, 8), :]
        q1[field, pl.ds(rows + 8, 8), :] = q1[field, pl.ds(8, 8), :]
    y_wait(ys.at[1], yr.at[1], 4)
    y_merge(yr.at[1], w)
    stencil(q1, xr.at[1], w, 1, f, inner, range(V))

    pair_sums(*on_modes(tuple(range(V)), f), inner, True)
    pair_sums(*on_duals(tuple(range(V)), f), inner, True)
    for n, fields in enumerate(fields_of):
        x_wait(xs.at[1], xr.at[1], fields, 12 + 2 * n)
        stencil(q1, xr.at[1], w, 1, f, outer, chunks[n])
    pair_sums(*on_modes(tuple(range(V)), f), outer, False)
    pair_sums(*on_duals(tuple(range(V)), f), outer, False)
    fold(0, PAIRS_UU)
    row2, sent2 = all_reduce(g2, lane_sums(), 1)
    spread(row2, 112, cb)

    def val(n):
        return cb[pl.ds(n, 1), :]

    c2 = [[val(V * m + i) for i in range(V)] for m in range(M)]
    ff, uf, dd = {}, {}, {}
    for n, (i, j) in enumerate(tri):
        ff[i, j] = val(PAIRS_FF + n)
    for m in range(M):
        for i in range(V):
            uf[m, i] = val(PAIRS_UF + V * m + i)
    for n, (i, j) in enumerate(uu):
        dd[i, j] = dd[j, i] = val(PAIRS_UU + n)

    gram = {}
    for j in range(V):
        h = [total_of(dd[m, n] * c2[n][j] for n in range(M)) - uf[m, j] for m in range(M)]
        for i in range(j, V):
            gram[i, j] = ff[j, i] + total_of(c2[m][i] * h[m] - c2[m][j] * uf[m, i] for m in range(M))
    low = {}
    inv = {}
    for j in range(V):
        pivot = gram[j, j]
        for k in range(j):
            pivot = pivot - low[j, k] * low[j, k]
        low[j, j] = jnp.sqrt(pivot)
        inv[j, j] = 1.0 / low[j, j]
        for i in range(j + 1, V):
            total = gram[i, j]
            for k in range(j):
                total = total - low[i, k] * low[j, k]
            low[i, j] = total * inv[j, j]
    for i in range(V):
        for j in range(i):
            total = low[i, j] * inv[j, j]
            for k in range(j + 1, i):
                total = total + low[i, k] * inv[k, j]
            inv[i, j] = -total * inv[i, i]
    lane1 = lax.broadcasted_iota(jnp.int32, (1, LN), 1)
    for i in range(V):
        row = jnp.zeros((1, LN), F32)
        for j in range(i + 1):
            row = jnp.where(lane1 == j, low[i, j], row)
        growth_ref[pl.ds(i, 1), :] = row[:, 0:V]
    scale = math.sqrt(cells)
    slot = {}
    n = 0
    for i in range(V):
        for j in range(i + 1):
            coef[pl.ds(n, 1), :] = scale * inv[i, j]
            slot["f", i, j] = n
            n += 1
    for i in range(V):
        for m in range(M):
            coef[pl.ds(n, 1), :] = -scale * total_of(inv[i, j] * c2[m][j] for j in range(i + 1))
            slot["u", i, m] = n
            n += 1

    for pick in ((0, 1), (2, 3)):
        weight = {
            key: jnp.broadcast_to(coef[pl.ds(n, 1), :], (8, LN)) for key, n in slot.items() if key[1] in pick
        }

        @pl.loop(0, rows // 8)
        def _(t):
            at = pl.ds(pl.multiple_of(8 * t, 8), 8)
            for c in range(C):
                fs = [f[C * i + c, at, :] for i in range(pick[-1] + 1)]
                us = [u[C * m + c, at, :] for m in range(M)]
                for i in pick:
                    terms = [weight["f", i, j] * fs[j] for j in range(i + 1)]
                    terms += [weight["u", i, m] * us[m] for m in range(M)]
                    out[C * i + c, at, :] = total_of(terms)

    for n in range(2):
        x_sent(bxs, bxr, snapshot[n], 2 * n)
    for n in range(2):
        x_sent(xs.at[0], xr.at[0], fields_of[n], 4 + 2 * n)
        x_sent(xs.at[1], xr.at[1], fields_of[n], 12 + 2 * n)
    sent1.wait_send()
    sent2.wait_send()
    y_sent(ys.at[0], yr.at[0], 0)
    y_sent(bys, byr, 2)
    y_sent(ys.at[1], yr.at[1], 4)


def body(n_gx, n_gy, adjoint_block, base_flow, direct_modes, dual_modes):
    nz = adjoint_block.shape[2]
    rows = nz * XL
    cells = float(C * nz * XL * n_gx * LN * n_gy)
    nf = V * C
    vm = lambda *shape: pltpu.VMEM(shape, F32)
    in_hbm = lambda array: pltpu.with_memory_space_constraint(array, pltpu.HBM)
    anyspace = pl.BlockSpec(memory_space=pltpu.HBM)
    out, growth = pl.pallas_call(
        functools.partial(kernel, n_gx, n_gy, nz, cells),
        name="adjoint_step",
        out_shape=(
            jax.ShapeDtypeStruct((nf, rows, LN), F32),
            jax.ShapeDtypeStruct((V, V), F32),
        ),
        in_specs=[anyspace] * 4,
        out_specs=(pl.BlockSpec(memory_space=pltpu.VMEM),) * 2,
        scratch_shapes=[
            vm(nf, rows + 16, LN), vm(2 * C, rows + 16, LN), vm(M * C, rows, LN), vm(M * C, rows, LN),
            vm(nf, rows, LN), vm(nf, rows + 16, LN), vm(nf, rows, LN),
            vm(2, 15, rows, LN), vm(PAIRS, 8, LN),
            vm(2, 2, nf, nz, LN), vm(2, 2, nf, nz, LN), vm(2, 2 * C, nz, LN), vm(2, 2 * C, nz, LN),
            vm(2, nz, LN), vm(2, 2, nz, LN), vm(nz, LN), vm(2, nz, LN), vm(nz, LN), vm(nz, LN),
            vm(LN, LN), vm(PAIRS_C, LN), vm(112, LN), vm(48, LN),
            vm(n_gx * n_gy, 1, LN), vm(n_gx * n_gy, 1, LN),
            pltpu.SemaphoreType.DMA((8,)),
            pltpu.SemaphoreType.DMA((20,)), pltpu.SemaphoreType.DMA((20,)),
            pltpu.SemaphoreType.DMA((6,)), pltpu.SemaphoreType.DMA((6,)),
            pltpu.SemaphoreType.DMA((2,)), pltpu.SemaphoreType.DMA((2,)), pltpu.SemaphoreType.REGULAR,
        ],
        compiler_params=pltpu.CompilerParams(
            collective_id=0, has_side_effects=True, vmem_limit_bytes=48 * 1024 * 1024
        ),
    )(
        in_hbm(adjoint_block.reshape(nf, rows, LN)),
        in_hbm(base_flow.reshape(2 * C, rows, LN)),
        in_hbm(direct_modes.reshape(M * C, rows, LN)),
        in_hbm(dual_modes.reshape(M * C, rows, LN)),
    )
    return out.reshape(adjoint_block.shape), growth


def solution(mesh):
    spec = P(None, None, None, "gx", "gy")
    return jax.shard_map(
        functools.partial(body, mesh.shape["gx"], mesh.shape["gy"]),
        mesh=mesh,
        in_specs=(spec,) * 4,
        out_specs=(spec, P()),
        check_vma=False,
    )
```

```python
import functools
import math

import jax
import jax.numpy as jnp
from jax import lax
from jax.experimental import pallas as pl
from jax.experimental.pallas import tpu as pltpu
from jax.sharding import PartitionSpec as P

MESH = pl.DeviceIdType.MESH
F32 = jnp.float32
STEP = 0.1
VISC = 0.2
V, C, M = 4, 3, 8
XL, LN = 4, 128
CHIPS_X = 4
PAIRS_C = 32
PAIRS_FF = 32
PAIRS_UF = 42
PAIRS_UU = 74
PAIRS = 110


def kernel(
    n_gx, n_gy, nz, cells,
    q_hbm, b_hbm, d_hbm, u_hbm, out, growth_ref,
    q, b, d, u, a1, q1, f, terms, part,
    xs, xr, bxs, bxr, ys, yr, bys, byr, w, wb,
    acc, ca, cb, coef, g1, g2,
    in_sem, sx_sem, rx_sem, sy_sem, ry_sem, sg_sem, rg_sem, known,
):
    rows = nz * XL
    blocks = nz // 8
    nf = V * C
    gx, gy = lax.axis_index("gx"), lax.axis_index("gy")
    core = lax.rem(gx, 2)
    cx = lax.rem(lax.div(gx, 2), CHIPS_X)
    cz = lax.div(gx, 2 * CHIPS_X)
    n_z = n_gx // (2 * CHIPS_X)

    def ring(size):
        return sorted(range(1, size), key=lambda s: -min(s, size - s)) + [0]

    zs = [lax.rem(cz + s, n_z) if s else cz for s in ring(n_z)]
    xs_ = [lax.rem(cx + s, CHIPS_X) if s else cx for s in ring(CHIPS_X)]
    ys_ = [lax.rem(gy + s, n_gy) if s else gy for s in ring(n_gy)]
    peers_z = [((z * CHIPS_X + cx) * 2 + c, gy) for z in zs for c in (1 - core, core)][:-1]
    peers_x = [((cz * CHIPS_X + x) * 2 + core, gy) for x in xs_][:-1]
    peers_y = [(gx, y) for y in ys_][:-1]
    peers_near = [
        p for s, p in zip([s for s in ring(n_z) for _ in range(2)], peers_z) if min(s, n_z - s) <= max(n_z // 4, 1)
    ]

    def hops(size, n):
        s = (ring(size))[n]
        return min(s, size - s)

    order = sorted(
        (
            (i, j, k, n)
            for i in range(n_z) for j in range(CHIPS_X) for k in range(n_gy) for n in range(2)
        ),
        key=lambda t: -(4 * (hops(n_z, t[0]) + hops(CHIPS_X, t[1]) + hops(n_gy, t[2])) + (t[3] == 0)),
    )[:-1]
    peers_all = [
        ((zs[i] * CHIPS_X + xs_[j]) * 2 + (1 - core if n == 0 else core), ys_[k]) for i, j, k, n in order
    ]

    left, right = (lax.rem(gx + n_gx - 1, n_gx), gy), (lax.rem(gx + 1, n_gx), gy)
    below, above = (gx, lax.rem(gy + n_gy - 1, n_gy)), (gx, lax.rem(gy + 1, n_gy))
    has_l, has_r = gx > 0, gx < n_gx - 1
    has_b, has_a = gy > 0, gy < n_gy - 1

    def total_of(terms):
        terms = list(terms)
        while len(terms) > 1:
            terms = [
                terms[i] + terms[i + 1] if i + 1 < len(terms) else terms[i] for i in range(0, len(terms), 2)
            ]
        return terms[0]

    q_main = pltpu.make_async_copy(q_hbm, q.at[:, pl.ds(8, rows), :], in_sem.at[0])
    q_low = pltpu.make_async_copy(q_hbm.at[:, pl.ds(rows - 8, 8), :], q.at[:, pl.ds(0, 8), :], in_sem.at[1])
    q_high = pltpu.make_async_copy(q_hbm.at[:, pl.ds(0, 8), :], q.at[:, pl.ds(rows + 8, 8), :], in_sem.at[2])
    b_main = pltpu.make_async_copy(b_hbm, b.at[:, pl.ds(8, rows), :], in_sem.at[3])
    b_low = pltpu.make_async_copy(b_hbm.at[:, pl.ds(rows - 8, 8), :], b.at[:, pl.ds(0, 8), :], in_sem.at[4])
    b_high = pltpu.make_async_copy(b_hbm.at[:, pl.ds(0, 8), :], b.at[:, pl.ds(rows + 8, 8), :], in_sem.at[5])
    u_main = pltpu.make_async_copy(u_hbm, u, in_sem.at[6])
    d_main = pltpu.make_async_copy(d_hbm, d, in_sem.at[7])
    q_main.start()
    b_main.start()
    for copy in (q_low, q_high, b_low, b_high, u_main, d_main):
        copy.start()

    barrier = pltpu.get_barrier_semaphore()
    for peer in (left, right, below, above):
        pl.semaphore_signal(barrier, inc=1, device_id=peer, device_id_type=MESH)

    for peer in peers_x + peers_y + peers_near:
        pl.semaphore_signal(barrier, inc=1, device_id=peer, device_id_type=MESH)

    lane = lax.broadcasted_iota(jnp.int32, (8, LN), 1)
    half = lax.shift_right_logical(lane, 1)
    first, final, odd = lane == 0, lane == LN - 1, lax.rem(lane, 2) == 1

    def plane(ref, field, k, x, dz=0, pad=8):
        return ref[field, pl.ds(pad + 8 * XL * k + x + XL * dz, 8, stride=XL), :]

    def zero(ref, count):
        @pl.loop(0, count)
        def _(i):
            ref[i] = jnp.zeros((nz, LN), F32)

    def x_copy(send, recv, fields, side, sem):
        peer = left if side == 0 else right
        return pltpu.make_async_remote_copy(
            src_ref=send.at[side, fields], dst_ref=recv.at[1 - side, fields],
            send_sem=sx_sem.at[sem + side], recv_sem=rx_sem.at[sem + 1 - side],
            device_id=peer, device_id_type=MESH,
        )

    def x_each(act):
        for side, there in ((0, has_l), (1, has_r)):
            @pl.when(there)
            def _():
                act(side)

    def x_start(send, recv, fields, sem):
        x_each(lambda side: x_copy(send, recv, fields, side, sem).start())

    def x_wait(send, recv, fields, sem):
        x_each(lambda side: x_copy(send, recv, fields, 1 - side, sem).wait_recv())

    def x_sent(send, recv, fields, sem):
        x_each(lambda side: x_copy(send, recv, fields, side, sem).wait_send())

    def x_zero(recv, count):
        for side, there in ((0, has_l), (1, has_r)):
            @pl.when(jnp.logical_not(there))
            def _():
                zero(recv.at[side], count)

    def y_copy(send, recv, side, sem):
        peer = below if side == 0 else above
        return pltpu.make_async_remote_copy(
            src_ref=send, dst_ref=recv.at[1 - side],
            send_sem=sy_sem.at[sem + side], recv_sem=ry_sem.at[sem + 1 - side],
            device_id=peer, device_id_type=MESH,
        )

    def y_start(send, recv, sem):
        for side, there in ((0, has_b), (1, has_a)):
            @pl.when(there)
            def _():
                y_copy(send, recv, side, sem).start()

    def y_wait(send, recv, sem):
        for side, there in ((0, has_b), (1, has_a)):
            @pl.when(there)
            def _():
                y_copy(send, recv, 1 - side, sem).wait_recv()

    def y_sent(send, recv, sem):
        for side, there in ((0, has_b), (1, has_a)):
            @pl.when(there)
            def _():
                y_copy(send, recv, side, sem).wait_send()

    def y_zero(recv):
        for side, there in ((0, has_b), (1, has_a)):
            @pl.when(jnp.logical_not(there))
            def _():
                recv[side] = jnp.zeros((nz, LN), F32)

    def x_pack(ref, send, count):
        @pl.loop(0, count)
        def _(i):
            for k in range(blocks):
                at = pl.ds(8 * k, 8)
                send[0, i, at, :] = plane(ref, i, k, 0)
                send[1, i, at, :] = plane(ref, i, k, XL - 1)

    def y_pack(ref, send, count):
        @pl.loop(0, blocks)
        def _(k):
            total = jnp.zeros((8, LN), F32)
            for x in range(XL):
                for i in range(count):
                    at = 16 * x + i
                    total = jnp.where(half == at, pltpu.roll(plane(ref, i, k, x), 2 * at + 1, 1), total)
            send[pl.ds(pl.multiple_of(8 * k, 8), 8), :] = total

    def y_merge(recv, merged):
        for k in range(blocks):
            at = pl.ds(8 * k, 8)
            merged[at, :] = jnp.where(
                odd, pltpu.roll(recv[0, at, :], 1, 1), pltpu.roll(recv[1, at, :], LN - 1, 1)
            )

    def beside_y(value, edges, x, field):
        fix = pltpu.roll(edges, LN - (32 * x + 2 * field + 1), 1)
        return (
            jnp.where(first, fix, pltpu.roll(value, 1, 1)),
            jnp.where(final, fix, pltpu.roll(value, LN - 1, 1)),
        )

    def beside_x(ref, recv, field, k, x):
        at = pl.ds(pl.multiple_of(8 * k, 8), 8)
        low = recv[0, field, at, :] if x == 0 else plane(ref, field, k, x - 1)
        high = recv[1, field, at, :] if x == XL - 1 else plane(ref, field, k, x + 1)
        return low, high

    def base_terms(s, planes):
        @pl.loop(0, blocks)
        def _(k):
            wbk = wb[pl.ds(pl.multiple_of(8 * k, 8), 8), :]
            for x in planes:
                at = pl.ds(pl.multiple_of(8 * k, 8) + nz * x, 8)
                mix = [[None] * C for _ in range(C)]
                for j in range(C):
                    field = 3 * s + j
                    mid = plane(b, field, k, x)
                    xm, xp = beside_x(b, bxr, field, k, x)
                    ym, yp = beside_y(mid, wbk, x, field)
                    zm, zp = plane(b, field, k, x, -1), plane(b, field, k, x, 1)
                    for c, (m_, p_) in enumerate(((xm, xp), (ym, yp), (zm, zp))):
                        mix[c][j] = 0.5 * STEP * (m_ - p_)
                    terms[s, 2 * j, at, :] = VISC * STEP - 0.5 * STEP * mid
                    terms[s, 2 * j + 1, at, :] = VISC * STEP + 0.5 * STEP * mid
                for c in range(C):
                    for j in range(C):
                        extra = 1.0 - 6.0 * VISC * STEP if c == j else 0.0
                        terms[s, 6 + C * c + j, at, :] = mix[c][j] + extra if extra else mix[c][j]

    def stencil(src, src_x, edges, s, dst, planes, vectors):
        @pl.loop(0, blocks)
        def _(k):
            wk = edges[pl.ds(pl.multiple_of(8 * k, 8), 8), :]
            for x in planes:
                at = pl.ds(pl.multiple_of(8 * k, 8) + nz * x, 8)
                side = [terms[s, n, at, :] for n in range(6)]
                mix = [[terms[s, 6 + C * c + j, at, :] for j in range(C)] for c in range(C)]
                for v in vectors:
                    mid = [plane(src, C * v + c, k, x) for c in range(C)]
                    for c in range(C):
                        field = C * v + c
                        xm, xp = beside_x(src, src_x, field, k, x)
                        ym, yp = beside_y(mid[c], wk, x, field)
                        zm, zp = plane(src, field, k, x, -1), plane(src, field, k, x, 1)
                        total = mix[c][0] * mid[0] + mix[c][1] * mid[1] + mix[c][2] * mid[2]
                        total = total + (side[0] * xm + side[1] * xp)
                        total = total + (side[2] * ym + side[3] * yp)
                        total = total + (side[4] * zm + side[5] * zp)
                        dst[field, pl.ds(8 * XL * k + x, 8, stride=XL), :] = total

    def pair_sums(pairs, loader, planes, fresh):
        def body(k, sums):
            sums = list(sums)
            for x in planes:
                at = pl.ds(8 * XL * k + x, 8, stride=XL)
                for c in range(C):
                    left_, right_ = loader(c, at)
                    for n, (_, i, j) in enumerate(pairs):
                        sums[n] = sums[n] + left_[i] * right_[j]
            return tuple(sums)

        begin = tuple(jnp.zeros((8, LN), F32) if fresh else part[n] for n, _, _ in pairs)
        for (n, _, _), value in zip(pairs, lax.fori_loop(0, blocks, body, begin)):
            part[n] = value

    def on_modes(vectors, field):
        pairs = [(V * m + i, m, n) for n, i in enumerate(vectors) for m in range(M)]

        def loader(c, at):
            return [d[C * m + c, at, :] for m in range(M)], [field[C * i + c, at, :] for i in vectors]

        return pairs, loader

    tri = [(i, j) for i in range(V) for j in range(i, V)]
    uu = [(i, j) for i in range(M) for j in range(i, M)]

    def on_duals(vectors, field):
        count = vectors[-1] + 1
        pairs = [(PAIRS_FF + n, M + i, j) for n, (i, j) in enumerate(tri) if j in vectors]
        pairs += [(PAIRS_UF + V * m + i, m, i) for m in range(M) for i in vectors]

        def loader(c, at):
            fs = [field[C * i + c, at, :] for i in range(count)]
            return [u[C * m + c, at, :] for m in range(M)] + fs, fs

        return pairs, loader

    def among_duals():
        def loader(c, at):
            both = [u[C * m + c, at, :] for m in range(M)]
            return both, both

        return [(PAIRS_UU + n, i, j) for n, (i, j) in enumerate(uu)], loader

    def fold(start, count):
        for n in range(start, start + count):
            acc[pl.ds(n, 1), :] = jnp.sum(part[n], axis=0, keepdims=True)

    ones = jnp.ones((8, LN), F32)

    def all_reduce(buf, row, sem, fill=None):
        me = gx * n_gy + gy
        size = n_gx * n_gy
        buf[me] = row

        def copy(rows_, peer):
            return pltpu.make_async_remote_copy(
                src_ref=buf.at[rows_], dst_ref=buf.at[rows_],
                send_sem=sg_sem.at[sem], recv_sem=rg_sem.at[sem],
                device_id=peer, device_id_type=MESH,
            )

        for peer in peers_all:
            copy(me, peer).start()
        if fill is not None:
            fill()
        copy(pl.ds(0, size - 1), peers_all[0]).wait_recv()
        sums = total_of([total_of(buf[i + k] for k in range(16)) for i in range(0, size, 16)])
        return sums, copy(pl.ds(0, size - 1), peers_all[0])

    def lane_sums():
        return lax.dot_general(
            ones, acc[...], (((1,), (1,)), ((), ())),
            precision=lax.Precision.HIGHEST, preferred_element_type=F32,
        )[0:1, :]

    def spread(row, count, dst):
        r = lax.broadcasted_iota(jnp.int32, (count, LN), 0)
        l = lax.broadcasted_iota(jnp.int32, (count, LN), 1)
        chosen = jnp.where(r == l, jnp.broadcast_to(row, (count, LN)), 0.0)
        dst[pl.ds(0, count), :] = lax.dot_general(
            chosen, jnp.ones((LN, LN), F32), (((1,), (0,)), ((), ())),
            precision=lax.Precision.HIGHEST, preferred_element_type=F32,
        )

    everything = (1, 2, 0, 3)
    inner, outer = (1, 2), (0, 3)
    chunks = ((0, 1), (2, 3))
    fields_of = [pl.ds(C * c[0], C * len(c)) for c in chunks]
    snapshot = [pl.ds(C * s, C) for s in range(2)]
    q_main.wait()
    b_main.wait()
    x_pack(q, xs.at[0], nf)
    x_pack(b, bxs, 2 * C)
    pl.semaphore_wait(barrier, 4 + len(peers_x) + len(peers_y) + len(peers_near))
    x_start(bxs, bxr, snapshot[0], 0)
    for n, fields in enumerate(fields_of):
        x_start(xs.at[0], xr.at[0], fields, 4 + 2 * n)
    x_start(bxs, bxr, snapshot[1], 2)
    for peer in peers_x + peers_near:
        pl.semaphore_signal(known.at[0], inc=1, device_id=peer, device_id_type=MESH)
    y_pack(b, bys, 2 * C)
    y_start(bys, byr, 2)
    y_pack(q, ys.at[0], nf)
    y_start(ys.at[0], yr.at[0], 0)
    acc[...] = jnp.zeros((LN, LN), F32)
    x_zero(xr.at[0], nf)
    x_zero(xr.at[1], nf)
    x_zero(bxr, 2 * C)
    y_zero(yr.at[0])
    y_zero(yr.at[1])
    y_zero(byr)
    for copy in (q_low, q_high, b_low, b_high):
        copy.wait()
    y_wait(bys, byr, 2)
    y_merge(byr, wb)
    base_terms(0, inner)
    y_wait(ys.at[0], yr.at[0], 0)
    y_merge(yr.at[0], w)
    stencil(q, xr.at[0], w, 0, a1, inner, range(V))
    pl.semaphore_wait(known.at[0], len(peers_x) + len(peers_near))
    for peer in peers_z:
        pl.semaphore_signal(known.at[1], inc=1, device_id=peer, device_id_type=MESH)
    d_main.wait()

    pair_sums(*on_modes(tuple(range(V)), a1), inner, True)
    x_wait(bxs, bxr, snapshot[0], 0)
    base_terms(0, outer)
    for n, fields in enumerate(fields_of):
        x_wait(xs.at[0], xr.at[0], fields, 4 + 2 * n)
        stencil(q, xr.at[0], w, 0, a1, outer, chunks[n])
        pair_sums(*on_modes(chunks[n], a1), outer, False)
    fold(0, PAIRS_C)

    def second_base():
        x_wait(bxs, bxr, snapshot[1], 2)
        base_terms(1, everything)

    def dual_products():
        u_main.wait()
        pair_sums(*among_duals(), everything, True)

    def shadow():
        second_base()
        dual_products()

    pl.semaphore_wait(known.at[1], len(peers_z))
    row1, sent1 = all_reduce(g1, lane_sums(), 0, shadow)
    fold(PAIRS_UU, len(uu))
    spread(row1, PAIRS_C, ca)

    def deflate(planes, vectors, send):
        weight = {
            (m, i): jnp.broadcast_to(ca[pl.ds(V * m + i, 1), :], (8, LN)) for m in range(M) for i in vectors
        }

        @pl.loop(0, blocks)
        def _(k):
            at = pl.ds(pl.multiple_of(8 * k, 8), 8)
            for c in range(C):
                for x in planes:
                    dual = [plane(u, C * m + c, k, x, 0, 0) for m in range(M)]
                    for i in vectors:
                        field = C * i + c
                        total = plane(a1, field, k, x, 0, 0) - total_of(weight[m, i] * dual[m] for m in range(M))
                        q1[field, pl.ds(8 + 8 * XL * k + x, 8, stride=XL), :] = total
                        if send:
                            xs[1, 0 if x == 0 else 1, field, at, :] = total

    for n, fields in enumerate(fields_of):
        deflate(outer, chunks[n], True)
        x_start(xs.at[1], xr.at[1], fields, 12 + 2 * n)
    deflate(inner, range(V), False)
    y_pack(q1, ys.at[1], nf)
    y_start(ys.at[1], yr.at[1], 4)
    for field in range(nf):
        q1[field, pl.ds(0, 8), :] = q1[field, pl.ds(rows, 8), :]
        q1[field, pl.ds(rows + 8, 8), :] = q1[field, pl.ds(8, 8), :]
    y_wait(ys.at[1], yr.at[1], 4)
    y_merge(yr.at[1], w)
    stencil(q1, xr.at[1], w, 1, f, inner, range(V))

    pair_sums(*on_modes(tuple(range(V)), f), inner, True)
    pair_sums(*on_duals(tuple(range(V)), f), inner, True)
    for n, fields in enumerate(fields_of):
        x_wait(xs.at[1], xr.at[1], fields, 12 + 2 * n)
        stencil(q1, xr.at[1], w, 1, f, outer, chunks[n])
        pair_sums(*on_modes(chunks[n], f), outer, False)
        pair_sums(*on_duals(chunks[n], f), outer, False)
    fold(0, PAIRS_UU)
    row2, sent2 = all_reduce(g2, lane_sums(), 1)
    spread(row2, 112, cb)

    def val(n):
        return cb[pl.ds(n, 1), :]

    c2 = [[val(V * m + i) for i in range(V)] for m in range(M)]
    ff, uf, dd = {}, {}, {}
    for n, (i, j) in enumerate(tri):
        ff[i, j] = val(PAIRS_FF + n)
    for m in range(M):
        for i in range(V):
            uf[m, i] = val(PAIRS_UF + V * m + i)
    for n, (i, j) in enumerate(uu):
        dd[i, j] = dd[j, i] = val(PAIRS_UU + n)

    gram = {}
    for j in range(V):
        h = [total_of(dd[m, n] * c2[n][j] for n in range(M)) - uf[m, j] for m in range(M)]
        for i in range(j, V):
            gram[i, j] = ff[j, i] + total_of(c2[m][i] * h[m] - c2[m][j] * uf[m, i] for m in range(M))
    low = {}
    inv = {}
    for j in range(V):
        pivot = gram[j, j]
        for k in range(j):
            pivot = pivot - low[j, k] * low[j, k]
        low[j, j] = jnp.sqrt(pivot)
        inv[j, j] = 1.0 / low[j, j]
        for i in range(j + 1, V):
            total = gram[i, j]
            for k in range(j):
                total = total - low[i, k] * low[j, k]
            low[i, j] = total * inv[j, j]
    for i in range(V):
        for j in range(i):
            total = low[i, j] * inv[j, j]
            for k in range(j + 1, i):
                total = total + low[i, k] * inv[k, j]
            inv[i, j] = -total * inv[i, i]
    lane1 = lax.broadcasted_iota(jnp.int32, (1, LN), 1)
    for i in range(V):
        row = jnp.zeros((1, LN), F32)
        for j in range(i + 1):
            row = jnp.where(lane1 == j, low[i, j], row)
        growth_ref[pl.ds(i, 1), :] = row[:, 0:V]
    scale = math.sqrt(cells)
    slot = {}
    n = 0
    for i in range(V):
        for j in range(i + 1):
            coef[pl.ds(n, 1), :] = scale * inv[i, j]
            slot["f", i, j] = n
            n += 1
    for i in range(V):
        for m in range(M):
            coef[pl.ds(n, 1), :] = -scale * total_of(inv[i, j] * c2[m][j] for j in range(i + 1))
            slot["u", i, m] = n
            n += 1

    for pick in ((0, 1), (2, 3)):
        weight = {
            key: jnp.broadcast_to(coef[pl.ds(n, 1), :], (8, LN)) for key, n in slot.items() if key[1] in pick
        }

        @pl.loop(0, rows // 8)
        def _(t):
            at = pl.ds(pl.multiple_of(8 * t, 8), 8)
            for c in range(C):
                fs = [f[C * i + c, at, :] for i in range(pick[-1] + 1)]
                us = [u[C * m + c, at, :] for m in range(M)]
                for i in pick:
                    terms = [weight["f", i, j] * fs[j] for j in range(i + 1)]
                    terms += [weight["u", i, m] * us[m] for m in range(M)]
                    out[C * i + c, at, :] = total_of(terms)

    for n in range(2):
        x_sent(bxs, bxr, snapshot[n], 2 * n)
    for n in range(2):
        x_sent(xs.at[0], xr.at[0], fields_of[n], 4 + 2 * n)
        x_sent(xs.at[1], xr.at[1], fields_of[n], 12 + 2 * n)
    sent1.wait_send()
    sent2.wait_send()
    y_sent(ys.at[0], yr.at[0], 0)
    y_sent(bys, byr, 2)
    y_sent(ys.at[1], yr.at[1], 4)


def body(n_gx, n_gy, adjoint_block, base_flow, direct_modes, dual_modes):
    nz = adjoint_block.shape[2]
    rows = nz * XL
    cells = float(C * nz * XL * n_gx * LN * n_gy)
    nf = V * C
    vm = lambda *shape: pltpu.VMEM(shape, F32)
    in_hbm = lambda array: pltpu.with_memory_space_constraint(array, pltpu.HBM)
    anyspace = pl.BlockSpec(memory_space=pltpu.HBM)
    out, growth = pl.pallas_call(
        functools.partial(kernel, n_gx, n_gy, nz, cells),
        name="adjoint_step",
        out_shape=(
            jax.ShapeDtypeStruct((nf, rows, LN), F32),
            jax.ShapeDtypeStruct((V, V), F32),
        ),
        in_specs=[anyspace] * 4,
        out_specs=(pl.BlockSpec(memory_space=pltpu.VMEM),) * 2,
        scratch_shapes=[
            vm(nf, rows + 16, LN), vm(2 * C, rows + 16, LN), vm(M * C, rows, LN), vm(M * C, rows, LN),
            vm(nf, rows, LN), vm(nf, rows + 16, LN), vm(nf, rows, LN),
            vm(2, 15, rows, LN), vm(PAIRS, 8, LN),
            vm(2, 2, nf, nz, LN), vm(2, 2, nf, nz, LN), vm(2, 2 * C, nz, LN), vm(2, 2 * C, nz, LN),
            vm(2, nz, LN), vm(2, 2, nz, LN), vm(nz, LN), vm(2, nz, LN), vm(nz, LN), vm(nz, LN),
            vm(LN, LN), vm(PAIRS_C, LN), vm(112, LN), vm(48, LN),
            vm(n_gx * n_gy, 1, LN), vm(n_gx * n_gy, 1, LN),
            pltpu.SemaphoreType.DMA((8,)),
            pltpu.SemaphoreType.DMA((20,)), pltpu.SemaphoreType.DMA((20,)),
            pltpu.SemaphoreType.DMA((6,)), pltpu.SemaphoreType.DMA((6,)),
            pltpu.SemaphoreType.DMA((2,)), pltpu.SemaphoreType.DMA((2,)), pltpu.SemaphoreType.REGULAR((2,)),
        ],
        compiler_params=pltpu.CompilerParams(
            collective_id=0, has_side_effects=True, vmem_limit_bytes=48 * 1024 * 1024
        ),
    )(
        in_hbm(adjoint_block.reshape(nf, rows, LN)),
        in_hbm(base_flow.reshape(2 * C, rows, LN)),
        in_hbm(direct_modes.reshape(M * C, rows, LN)),
        in_hbm(dual_modes.reshape(M * C, rows, LN)),
    )
    return out.reshape(adjoint_block.shape), growth


def solution(mesh):
    spec = P(None, None, None, "gx", "gy")
    return jax.shard_map(
        functools.partial(body, mesh.shape["gx"], mesh.shape["gy"]),
        mesh=mesh,
        in_specs=(spec,) * 4,
        out_specs=(spec, P()),
        check_vma=False,
    )
```

```python
import functools
import math

import jax
import jax.numpy as jnp
from jax import lax
from jax.experimental import pallas as pl
from jax.experimental.pallas import tpu as pltpu
from jax.sharding import PartitionSpec as P

MESH = pl.DeviceIdType.MESH
F32 = jnp.float32
STEP = 0.1
VISC = 0.2
V, C, M = 4, 3, 8
XL, LN = 4, 128
CHIPS_X = 4
PAIRS_C = 32
PAIRS_FF = 32
PAIRS_UF = 42
PAIRS_UU = 74
PAIRS = 110


def kernel(
    n_gx, n_gy, nz, cells,
    q_hbm, b_hbm, d_hbm, u_hbm, out, growth_ref,
    q, b, d, u, a1, q1, f, terms, part,
    xs, xr, bxs, bxr, ys, yr, bys, byr, w, wb,
    acc, ca, cb, coef, g1, g2,
    in_sem, sx_sem, rx_sem, sy_sem, ry_sem, sg_sem, rg_sem, known,
):
    rows = nz * XL
    blocks = nz // 8
    nf = V * C
    gx, gy = lax.axis_index("gx"), lax.axis_index("gy")
    core = lax.rem(gx, 2)
    cx = lax.rem(lax.div(gx, 2), CHIPS_X)
    cz = lax.div(gx, 2 * CHIPS_X)
    n_z = n_gx // (2 * CHIPS_X)

    def ring(size):
        return sorted(range(1, size), key=lambda s: -min(s, size - s)) + [0]

    zs = [lax.rem(cz + s, n_z) if s else cz for s in ring(n_z)]
    xs_ = [lax.rem(cx + s, CHIPS_X) if s else cx for s in ring(CHIPS_X)]
    ys_ = [lax.rem(gy + s, n_gy) if s else gy for s in ring(n_gy)]
    peers_z = [((z * CHIPS_X + cx) * 2 + c, gy) for z in zs for c in (1 - core, core)][:-1]
    peers_x = [((cz * CHIPS_X + x) * 2 + core, gy) for x in xs_][:-1]
    peers_y = [(gx, y) for y in ys_][:-1]
    peers_near = [
        p for s, p in zip([s for s in ring(n_z) for _ in range(2)], peers_z) if min(s, n_z - s) <= max(n_z // 4, 1)
    ]

    def hops(size, n):
        s = (ring(size))[n]
        return min(s, size - s)

    order = sorted(
        (
            (i, j, k, n)
            for i in range(n_z) for j in range(CHIPS_X) for k in range(n_gy) for n in range(2)
        ),
        key=lambda t: -(4 * (hops(n_z, t[0]) + hops(CHIPS_X, t[1]) + hops(n_gy, t[2])) + (t[3] == 0)),
    )[:-1]
    peers_all = [
        ((zs[i] * CHIPS_X + xs_[j]) * 2 + (1 - core if n == 0 else core), ys_[k]) for i, j, k, n in order
    ]

    left, right = (lax.rem(gx + n_gx - 1, n_gx), gy), (lax.rem(gx + 1, n_gx), gy)
    below, above = (gx, lax.rem(gy + n_gy - 1, n_gy)), (gx, lax.rem(gy + 1, n_gy))
    has_l, has_r = gx > 0, gx < n_gx - 1
    has_b, has_a = gy > 0, gy < n_gy - 1

    def total_of(terms):
        terms = list(terms)
        while len(terms) > 1:
            terms = [
                terms[i] + terms[i + 1] if i + 1 < len(terms) else terms[i] for i in range(0, len(terms), 2)
            ]
        return terms[0]

    q_main = pltpu.make_async_copy(q_hbm, q.at[:, pl.ds(8, rows), :], in_sem.at[0])
    q_low = pltpu.make_async_copy(q_hbm.at[:, pl.ds(rows - 8, 8), :], q.at[:, pl.ds(0, 8), :], in_sem.at[1])
    q_high = pltpu.make_async_copy(q_hbm.at[:, pl.ds(0, 8), :], q.at[:, pl.ds(rows + 8, 8), :], in_sem.at[2])
    b_main = pltpu.make_async_copy(b_hbm, b.at[:, pl.ds(8, rows), :], in_sem.at[3])
    b_low = pltpu.make_async_copy(b_hbm.at[:, pl.ds(rows - 8, 8), :], b.at[:, pl.ds(0, 8), :], in_sem.at[4])
    b_high = pltpu.make_async_copy(b_hbm.at[:, pl.ds(0, 8), :], b.at[:, pl.ds(rows + 8, 8), :], in_sem.at[5])
    u_main = pltpu.make_async_copy(u_hbm, u, in_sem.at[6])
    d_main = pltpu.make_async_copy(d_hbm, d, in_sem.at[7])
    q_main.start()
    b_main.start()
    for copy in (q_low, q_high, b_low, b_high, u_main, d_main):
        copy.start()

    barrier = pltpu.get_barrier_semaphore()
    for peer in (left, right, below, above):
        pl.semaphore_signal(barrier, inc=1, device_id=peer, device_id_type=MESH)

    for peer in peers_x + peers_y + peers_near:
        pl.semaphore_signal(barrier, inc=1, device_id=peer, device_id_type=MESH)

    lane = lax.broadcasted_iota(jnp.int32, (8, LN), 1)
    half = lax.shift_right_logical(lane, 1)
    first, final, odd = lane == 0, lane == LN - 1, lax.rem(lane, 2) == 1

    def plane(ref, field, k, x, dz=0, pad=8):
        return ref[field, pl.ds(pad + 8 * XL * k + x + XL * dz, 8, stride=XL), :]

    def zero(ref, count):
        @pl.loop(0, count)
        def _(i):
            ref[i] = jnp.zeros((nz, LN), F32)

    def x_copy(send, recv, fields, side, sem):
        peer = left if side == 0 else right
        return pltpu.make_async_remote_copy(
            src_ref=send.at[side, fields], dst_ref=recv.at[1 - side, fields],
            send_sem=sx_sem.at[sem + side], recv_sem=rx_sem.at[sem + 1 - side],
            device_id=peer, device_id_type=MESH,
        )

    def x_each(act):
        for side, there in ((0, has_l), (1, has_r)):
            @pl.when(there)
            def _():
                act(side)

    def x_start(send, recv, fields, sem):
        x_each(lambda side: x_copy(send, recv, fields, side, sem).start())

    def x_wait(send, recv, fields, sem):
        x_each(lambda side: x_copy(send, recv, fields, 1 - side, sem).wait_recv())

    def x_sent(send, recv, fields, sem):
        x_each(lambda side: x_copy(send, recv, fields, side, sem).wait_send())

    def x_zero(recv, count):
        for side, there in ((0, has_l), (1, has_r)):
            @pl.when(jnp.logical_not(there))
            def _():
                zero(recv.at[side], count)

    def y_copy(send, recv, side, sem):
        peer = below if side == 0 else above
        return pltpu.make_async_remote_copy(
            src_ref=send, dst_ref=recv.at[1 - side],
            send_sem=sy_sem.at[sem + side], recv_sem=ry_sem.at[sem + 1 - side],
            device_id=peer, device_id_type=MESH,
        )

    def y_start(send, recv, sem):
        for side, there in ((0, has_b), (1, has_a)):
            @pl.when(there)
            def _():
                y_copy(send, recv, side, sem).start()

    def y_wait(send, recv, sem):
        for side, there in ((0, has_b), (1, has_a)):
            @pl.when(there)
            def _():
                y_copy(send, recv, 1 - side, sem).wait_recv()

    def y_sent(send, recv, sem):
        for side, there in ((0, has_b), (1, has_a)):
            @pl.when(there)
            def _():
                y_copy(send, recv, side, sem).wait_send()

    def y_zero(recv):
        for side, there in ((0, has_b), (1, has_a)):
            @pl.when(jnp.logical_not(there))
            def _():
                recv[side] = jnp.zeros((nz, LN), F32)

    def x_pack(ref, send, count):
        @pl.loop(0, count)
        def _(i):
            for k in range(blocks):
                at = pl.ds(8 * k, 8)
                send[0, i, at, :] = plane(ref, i, k, 0)
                send[1, i, at, :] = plane(ref, i, k, XL - 1)

    def y_pack(ref, send, count):
        @pl.loop(0, blocks)
        def _(k):
            total = jnp.zeros((8, LN), F32)
            for x in range(XL):
                for i in range(count):
                    at = 16 * x + i
                    total = jnp.where(half == at, pltpu.roll(plane(ref, i, k, x), 2 * at + 1, 1), total)
            send[pl.ds(pl.multiple_of(8 * k, 8), 8), :] = total

    def y_merge(recv, merged):
        for k in range(blocks):
            at = pl.ds(8 * k, 8)
            merged[at, :] = jnp.where(
                odd, pltpu.roll(recv[0, at, :], 1, 1), pltpu.roll(recv[1, at, :], LN - 1, 1)
            )

    def beside_y(value, edges, x, field):
        fix = pltpu.roll(edges, LN - (32 * x + 2 * field + 1), 1)
        return (
            jnp.where(first, fix, pltpu.roll(value, 1, 1)),
            jnp.where(final, fix, pltpu.roll(value, LN - 1, 1)),
        )

    def beside_x(ref, recv, field, k, x):
        at = pl.ds(pl.multiple_of(8 * k, 8), 8)
        low = recv[0, field, at, :] if x == 0 else plane(ref, field, k, x - 1)
        high = recv[1, field, at, :] if x == XL - 1 else plane(ref, field, k, x + 1)
        return low, high

    def base_terms(s, planes):
        @pl.loop(0, blocks)
        def _(k):
            wbk = wb[pl.ds(pl.multiple_of(8 * k, 8), 8), :]
            for x in planes:
                at = pl.ds(pl.multiple_of(8 * k, 8) + nz * x, 8)
                mix = [[None] * C for _ in range(C)]
                for j in range(C):
                    field = 3 * s + j
                    mid = plane(b, field, k, x)
                    xm, xp = beside_x(b, bxr, field, k, x)
                    ym, yp = beside_y(mid, wbk, x, field)
                    zm, zp = plane(b, field, k, x, -1), plane(b, field, k, x, 1)
                    for c, (m_, p_) in enumerate(((xm, xp), (ym, yp), (zm, zp))):
                        mix[c][j] = 0.5 * STEP * (m_ - p_)
                    terms[s, 2 * j, at, :] = VISC * STEP - 0.5 * STEP * mid
                    terms[s, 2 * j + 1, at, :] = VISC * STEP + 0.5 * STEP * mid
                for c in range(C):
                    for j in range(C):
                        extra = 1.0 - 6.0 * VISC * STEP if c == j else 0.0
                        terms[s, 6 + C * c + j, at, :] = mix[c][j] + extra if extra else mix[c][j]

    def stencil(src, src_x, edges, s, dst, planes, vectors):
        @pl.loop(0, blocks)
        def _(k):
            wk = edges[pl.ds(pl.multiple_of(8 * k, 8), 8), :]
            for x in planes:
                at = pl.ds(pl.multiple_of(8 * k, 8) + nz * x, 8)
                side = [terms[s, n, at, :] for n in range(6)]
                mix = [[terms[s, 6 + C * c + j, at, :] for j in range(C)] for c in range(C)]
                for v in vectors:
                    mid = [plane(src, C * v + c, k, x) for c in range(C)]
                    for c in range(C):
                        field = C * v + c
                        xm, xp = beside_x(src, src_x, field, k, x)
                        ym, yp = beside_y(mid[c], wk, x, field)
                        zm, zp = plane(src, field, k, x, -1), plane(src, field, k, x, 1)
                        total = mix[c][0] * mid[0] + mix[c][1] * mid[1] + mix[c][2] * mid[2]
                        total = total + (side[0] * xm + side[1] * xp)
                        total = total + (side[2] * ym + side[3] * yp)
                        total = total + (side[4] * zm + side[5] * zp)
                        dst[field, pl.ds(8 * XL * k + x, 8, stride=XL), :] = total

    def pair_sums(pairs, loader, planes, fresh):
        def body(k, sums):
            sums = list(sums)
            for x in planes:
                at = pl.ds(8 * XL * k + x, 8, stride=XL)
                for c in range(C):
                    left_, right_ = loader(c, at)
                    for n, (_, i, j) in enumerate(pairs):
                        sums[n] = sums[n] + left_[i] * right_[j]
            return tuple(sums)

        begin = tuple(jnp.zeros((8, LN), F32) if fresh else part[n] for n, _, _ in pairs)
        for (n, _, _), value in zip(pairs, lax.fori_loop(0, blocks, body, begin)):
            part[n] = value

    def on_modes(vectors, field):
        pairs = [(V * m + i, m, n) for n, i in enumerate(vectors) for m in range(M)]

        def loader(c, at):
            return [d[C * m + c, at, :] for m in range(M)], [field[C * i + c, at, :] for i in vectors]

        return pairs, loader

    tri = [(i, j) for i in range(V) for j in range(i, V)]
    uu = [(i, j) for i in range(M) for j in range(i, M)]

    def on_duals(vectors, field):
        count = vectors[-1] + 1
        pairs = [(PAIRS_FF + n, M + i, j) for n, (i, j) in enumerate(tri) if j in vectors]
        pairs += [(PAIRS_UF + V * m + i, m, i) for m in range(M) for i in vectors]

        def loader(c, at):
            fs = [field[C * i + c, at, :] for i in range(count)]
            return [u[C * m + c, at, :] for m in range(M)] + fs, fs

        return pairs, loader

    def among_duals():
        def loader(c, at):
            both = [u[C * m + c, at, :] for m in range(M)]
            return both, both

        return [(PAIRS_UU + n, i, j) for n, (i, j) in enumerate(uu)], loader

    def fold(start, count):
        for n in range(start, start + count):
            acc[pl.ds(n, 1), :] = jnp.sum(part[n], axis=0, keepdims=True)

    def all_reduce(buf, row, sem, fill=None):
        me = gx * n_gy + gy
        size = n_gx * n_gy
        buf[me] = row

        def copy(rows_, peer):
            return pltpu.make_async_remote_copy(
                src_ref=buf.at[rows_], dst_ref=buf.at[rows_],
                send_sem=sg_sem.at[sem], recv_sem=rg_sem.at[sem],
                device_id=peer, device_id_type=MESH,
            )

        for peer in peers_all:
            copy(me, peer).start()
        if fill is not None:
            fill()
        copy(pl.ds(0, size - 1), peers_all[0]).wait_recv()
        sums = total_of([total_of(buf[i + k] for k in range(16)) for i in range(0, size, 16)])
        return sums, copy(pl.ds(0, size - 1), peers_all[0])

    def eye(count):
        r = lax.broadcasted_iota(jnp.int32, (count, LN), 0)
        return r == lax.broadcasted_iota(jnp.int32, (count, LN), 1)

    def lane_sums(count):
        sums = jnp.sum(acc[pl.ds(0, count), :], axis=1, keepdims=True)
        return jnp.sum(jnp.where(eye(count), sums, 0.0), axis=0, keepdims=True)

    def spread(row, count, dst):
        chosen = jnp.where(eye(count), jnp.broadcast_to(row, (count, LN)), 0.0)
        dst[pl.ds(0, count), :] = jnp.broadcast_to(jnp.sum(chosen, axis=1, keepdims=True), (count, LN))

    everything = (1, 2, 0, 3)
    inner, outer = (1, 2), (0, 3)
    chunks = ((0, 1), (2, 3))
    fields_of = [pl.ds(C * c[0], C * len(c)) for c in chunks]
    snapshot = [pl.ds(C * s, C) for s in range(2)]
    q_main.wait()
    b_main.wait()
    x_pack(q, xs.at[0], nf)
    x_pack(b, bxs, 2 * C)
    pl.semaphore_wait(barrier, 4 + len(peers_x) + len(peers_y) + len(peers_near))
    x_start(bxs, bxr, snapshot[0], 0)
    for n, fields in enumerate(fields_of):
        x_start(xs.at[0], xr.at[0], fields, 4 + 2 * n)
    x_start(bxs, bxr, snapshot[1], 2)
    for peer in peers_x + peers_near:
        pl.semaphore_signal(known.at[0], inc=1, device_id=peer, device_id_type=MESH)
    y_pack(b, bys, 2 * C)
    y_start(bys, byr, 2)
    y_pack(q, ys.at[0], nf)
    y_start(ys.at[0], yr.at[0], 0)
    acc[...] = jnp.zeros((LN, LN), F32)
    x_zero(xr.at[0], nf)
    x_zero(xr.at[1], nf)
    x_zero(bxr, 2 * C)
    y_zero(yr.at[0])
    y_zero(yr.at[1])
    y_zero(byr)
    for copy in (q_low, q_high, b_low, b_high):
        copy.wait()
    y_wait(bys, byr, 2)
    y_merge(byr, wb)
    base_terms(0, inner)
    y_wait(ys.at[0], yr.at[0], 0)
    y_merge(yr.at[0], w)
    stencil(q, xr.at[0], w, 0, a1, inner, range(V))
    pl.semaphore_wait(known.at[0], len(peers_x) + len(peers_near))
    for peer in peers_z:
        pl.semaphore_signal(known.at[1], inc=1, device_id=peer, device_id_type=MESH)
    d_main.wait()

    pair_sums(*on_modes(tuple(range(V)), a1), inner, True)
    x_wait(bxs, bxr, snapshot[0], 0)
    base_terms(0, outer)
    for n, fields in enumerate(fields_of):
        x_wait(xs.at[0], xr.at[0], fields, 4 + 2 * n)
        stencil(q, xr.at[0], w, 0, a1, outer, chunks[n])
        pair_sums(*on_modes(chunks[n], a1), outer, False)
    fold(0, PAIRS_C)

    def second_base():
        x_wait(bxs, bxr, snapshot[1], 2)
        base_terms(1, everything)

    def dual_products():
        u_main.wait()
        pair_sums(*among_duals(), everything, True)

    def shadow():
        second_base()
        dual_products()

    pl.semaphore_wait(known.at[1], len(peers_z))
    row1, sent1 = all_reduce(g1, lane_sums(PAIRS_C), 0, shadow)
    fold(PAIRS_UU, len(uu))
    spread(row1, PAIRS_C, ca)

    def deflate(planes, vectors, send):
        weight = {
            (m, i): jnp.broadcast_to(ca[pl.ds(V * m + i, 1), :], (8, LN)) for m in range(M) for i in vectors
        }

        @pl.loop(0, blocks)
        def _(k):
            at = pl.ds(pl.multiple_of(8 * k, 8), 8)
            for c in range(C):
                for x in planes:
                    dual = [plane(u, C * m + c, k, x, 0, 0) for m in range(M)]
                    for i in vectors:
                        field = C * i + c
                        total = plane(a1, field, k, x, 0, 0) - total_of(weight[m, i] * dual[m] for m in range(M))
                        q1[field, pl.ds(8 + 8 * XL * k + x, 8, stride=XL), :] = total
                        if send:
                            xs[1, 0 if x == 0 else 1, field, at, :] = total

    for n, fields in enumerate(fields_of):
        deflate(outer, chunks[n], True)
        x_start(xs.at[1], xr.at[1], fields, 12 + 2 * n)
    deflate(inner, range(V), False)
    y_pack(q1, ys.at[1], nf)
    y_start(ys.at[1], yr.at[1], 4)
    for field in range(nf):
        q1[field, pl.ds(0, 8), :] = q1[field, pl.ds(rows, 8), :]
        q1[field, pl.ds(rows + 8, 8), :] = q1[field, pl.ds(8, 8), :]
    y_wait(ys.at[1], yr.at[1], 4)
    y_merge(yr.at[1], w)
    stencil(q1, xr.at[1], w, 1, f, inner, range(V))

    pair_sums(*on_modes(tuple(range(V)), f), inner, True)
    pair_sums(*on_duals(tuple(range(V)), f), inner, True)
    for n, fields in enumerate(fields_of):
        x_wait(xs.at[1], xr.at[1], fields, 12 + 2 * n)
        stencil(q1, xr.at[1], w, 1, f, outer, chunks[n])
        pair_sums(*on_modes(chunks[n], f), outer, False)
        pair_sums(*on_duals(chunks[n], f), outer, False)
    fold(0, PAIRS_UU)
    row2, sent2 = all_reduce(g2, lane_sums(112), 1)
    spread(row2, 112, cb)

    def val(n):
        return cb[pl.ds(n, 1), :]

    c2 = [[val(V * m + i) for i in range(V)] for m in range(M)]
    ff, uf, dd = {}, {}, {}
    for n, (i, j) in enumerate(tri):
        ff[i, j] = val(PAIRS_FF + n)
    for m in range(M):
        for i in range(V):
            uf[m, i] = val(PAIRS_UF + V * m + i)
    for n, (i, j) in enumerate(uu):
        dd[i, j] = dd[j, i] = val(PAIRS_UU + n)

    gram = {}
    for j in range(V):
        h = [total_of(dd[m, n] * c2[n][j] for n in range(M)) - uf[m, j] for m in range(M)]
        for i in range(j, V):
            gram[i, j] = ff[j, i] + total_of(c2[m][i] * h[m] - c2[m][j] * uf[m, i] for m in range(M))
    low = {}
    inv = {}
    for j in range(V):
        pivot = gram[j, j]
        for k in range(j):
            pivot = pivot - low[j, k] * low[j, k]
        low[j, j] = jnp.sqrt(pivot)
        inv[j, j] = 1.0 / low[j, j]
        for i in range(j + 1, V):
            total = gram[i, j]
            for k in range(j):
                total = total - low[i, k] * low[j, k]
            low[i, j] = total * inv[j, j]
    for i in range(V):
        for j in range(i):
            total = low[i, j] * inv[j, j]
            for k in range(j + 1, i):
                total = total + low[i, k] * inv[k, j]
            inv[i, j] = -total * inv[i, i]
    lane1 = lax.broadcasted_iota(jnp.int32, (1, LN), 1)
    for i in range(V):
        row = jnp.zeros((1, LN), F32)
        for j in range(i + 1):
            row = jnp.where(lane1 == j, low[i, j], row)
        growth_ref[pl.ds(i, 1), :] = row[:, 0:V]
    scale = math.sqrt(cells)
    slot = {}
    n = 0
    for i in range(V):
        for j in range(i + 1):
            coef[pl.ds(n, 1), :] = scale * inv[i, j]
            slot["f", i, j] = n
            n += 1
    for i in range(V):
        for m in range(M):
            coef[pl.ds(n, 1), :] = -scale * total_of(inv[i, j] * c2[m][j] for j in range(i + 1))
            slot["u", i, m] = n
            n += 1

    for pick in ((0, 1), (2, 3)):
        weight = {
            key: jnp.broadcast_to(coef[pl.ds(n, 1), :], (8, LN)) for key, n in slot.items() if key[1] in pick
        }

        @pl.loop(0, rows // 8)
        def _(t):
            at = pl.ds(pl.multiple_of(8 * t, 8), 8)
            for c in range(C):
                fs = [f[C * i + c, at, :] for i in range(pick[-1] + 1)]
                us = [u[C * m + c, at, :] for m in range(M)]
                for i in pick:
                    terms = [weight["f", i, j] * fs[j] for j in range(i + 1)]
                    terms += [weight["u", i, m] * us[m] for m in range(M)]
                    out[C * i + c, at, :] = total_of(terms)

    for n in range(2):
        x_sent(bxs, bxr, snapshot[n], 2 * n)
    for n in range(2):
        x_sent(xs.at[0], xr.at[0], fields_of[n], 4 + 2 * n)
        x_sent(xs.at[1], xr.at[1], fields_of[n], 12 + 2 * n)
    sent1.wait_send()
    sent2.wait_send()
    y_sent(ys.at[0], yr.at[0], 0)
    y_sent(bys, byr, 2)
    y_sent(ys.at[1], yr.at[1], 4)


def body(n_gx, n_gy, adjoint_block, base_flow, direct_modes, dual_modes):
    nz = adjoint_block.shape[2]
    rows = nz * XL
    cells = float(C * nz * XL * n_gx * LN * n_gy)
    nf = V * C
    vm = lambda *shape: pltpu.VMEM(shape, F32)
    in_hbm = lambda array: pltpu.with_memory_space_constraint(array, pltpu.HBM)
    anyspace = pl.BlockSpec(memory_space=pltpu.HBM)
    out, growth = pl.pallas_call(
        functools.partial(kernel, n_gx, n_gy, nz, cells),
        name="adjoint_step",
        out_shape=(
            jax.ShapeDtypeStruct((nf, rows, LN), F32),
            jax.ShapeDtypeStruct((V, V), F32),
        ),
        in_specs=[anyspace] * 4,
        out_specs=(pl.BlockSpec(memory_space=pltpu.VMEM),) * 2,
        scratch_shapes=[
            vm(nf, rows + 16, LN), vm(2 * C, rows + 16, LN), vm(M * C, rows, LN), vm(M * C, rows, LN),
            vm(nf, rows, LN), vm(nf, rows + 16, LN), vm(nf, rows, LN),
            vm(2, 15, rows, LN), vm(PAIRS, 8, LN),
            vm(2, 2, nf, nz, LN), vm(2, 2, nf, nz, LN), vm(2, 2 * C, nz, LN), vm(2, 2 * C, nz, LN),
            vm(2, nz, LN), vm(2, 2, nz, LN), vm(nz, LN), vm(2, nz, LN), vm(nz, LN), vm(nz, LN),
            vm(LN, LN), vm(PAIRS_C, LN), vm(112, LN), vm(48, LN),
            vm(n_gx * n_gy, 1, LN), vm(n_gx * n_gy, 1, LN),
            pltpu.SemaphoreType.DMA((8,)),
            pltpu.SemaphoreType.DMA((20,)), pltpu.SemaphoreType.DMA((20,)),
            pltpu.SemaphoreType.DMA((6,)), pltpu.SemaphoreType.DMA((6,)),
            pltpu.SemaphoreType.DMA((2,)), pltpu.SemaphoreType.DMA((2,)), pltpu.SemaphoreType.REGULAR((2,)),
        ],
        compiler_params=pltpu.CompilerParams(
            collective_id=0, has_side_effects=True, vmem_limit_bytes=48 * 1024 * 1024
        ),
    )(
        in_hbm(adjoint_block.reshape(nf, rows, LN)),
        in_hbm(base_flow.reshape(2 * C, rows, LN)),
        in_hbm(direct_modes.reshape(M * C, rows, LN)),
        in_hbm(dual_modes.reshape(M * C, rows, LN)),
    )
    return out.reshape(adjoint_block.shape), growth


def solution(mesh):
    spec = P(None, None, None, "gx", "gy")
    return jax.shard_map(
        functools.partial(body, mesh.shape["gx"], mesh.shape["gy"]),
        mesh=mesh,
        in_specs=(spec,) * 4,
        out_specs=(spec, P()),
        check_vma=False,
    )
```
